128 devices in a mesh: tm: 2 (over core), rows: 64 (over z, x, y).
Axes of the slice: x: 4, y: 4, z: 4, core: 2. Of those that a mesh axis runs over, the one named last changes fastest.
Arguments:
- feat: bfloat16 [4, 128, 240, 512], P('tm', 'rows'), may hold values from -24 to 24
- norm1_gain: float32 [512], replicated, may hold values from 0.5 to 1.5
- norm1_bias: float32 [512], replicated, may hold values from -3 to 3
- conv_weight: bfloat16 [3, 3, 3, 512, 512], replicated, may hold values from -0.0546875 to 0.0546875
- conv_bias: float32 [512], replicated, may hold values from -3 to 3
- norm2_gain: float32 [512], replicated, may hold values from 0.5 to 1.5
- norm2_bias: float32 [512], replicated, may hold values from -3 to 3
- w_query: bfloat16 [512, 512], replicated, may hold values from -0.44194174 to 0.44194174
- w_key: bfloat16 [512, 512], replicated, may hold values from -1.5467961 to 1.5467961
- w_value: bfloat16 [512, 512], replicated, may hold values from -0.25 to 0.25
- w_out: bfloat16 [512, 512], replicated, may hold values from -0.25 to 0.25
- out_bias: float32 [512], replicated, may hold values from -3 to 3
Outputs:
- block_out: bfloat16 [4, 128, 240, 512], P('tm', 'rows')
The draws below stay inside these ranges and needn't reach their ends.
All inputs are finite; a program needn't handle non-finite values.
Results may differ from the reference program's by a relative error of at most 0.0062.
The reference program's roundings to bfloat16 on the way (of `act`, `resid`, `normed`, `query`, `weight` and `attn`) count: a program that leaves them out, or rounds other values in their place, can miss the bound.
Values may be sent and summed in bfloat16 or wider, within the bound.
No kernel may reach another device: no remote copies, remote signals or barrier semaphores. Data moves between devices by JAX's collectives and lax.ppermute only.
A program may use at most 128 MiB of HBM per device.

```python
import math
import jax
import jax.numpy as jnp
from jax import lax

C = 512
GROUPS = 32
ROWS_DEV = 2
W = 240
RADIUS = 4
FR = 4
H = 128
N_ROWS = 64


def draw_feat(key, part):
    first = jax.random.fold_in(key, 31)
    second = jax.random.fold_in(key, 32)
    fourth = jax.random.fold_in(key, 34)
    fifth = jax.random.fold_in(key, 35)
    rows_float = jnp.arange(H, dtype=jnp.float32) / (H - 1)
    ramp = 1.0 + 2.0 * rows_float
    offset = jnp.clip(0.5 * jax.random.normal(second, (C,), jnp.float32), -2.0, 2.0)
    stripe_shift = jnp.repeat(jax.random.uniform(fourth, (H // ROWS_DEV,), jnp.float32, -5.0, 5.0), ROWS_DEV)
    frame_shift = jax.random.uniform(fifth, (FR,), jnp.float32, -2.0, 2.0)
    shifts = stripe_shift[None, :, None, None] + frame_shift[:, None, None, None]
    base = jnp.clip(jax.random.normal(first, (FR, H, W, C), jnp.float32), -5.0, 5.0)
    rising = 0.5 + 2.0 * rows_float
    values = base * ramp[None, :, None, None] + offset + rising[None, :, None, None] + shifts
    values = jnp.clip(values, -24.0, 24.0)
    return values.astype(jnp.bfloat16)


def query_key(key):
    base = jnp.clip(jax.random.normal(jax.random.fold_in(key, 11), (C, C), jnp.float32), -5.0, 5.0)
    noise = jnp.clip(jax.random.normal(jax.random.fold_in(key, 12), (C, C), jnp.float32), -5.0, 5.0)
    base = 2.0 * base / math.sqrt(C)
    noise = noise / math.sqrt(C)
    return (base, noise)


def draw_w_query(key, part):
    return query_key(key)[0].astype(jnp.bfloat16)


def draw_w_key(key, part):
    return query_key(key)[1].astype(jnp.bfloat16)


def gaussian(own_key, dims, deviation, most, kind=jnp.bfloat16):
    result = jax.random.normal(own_key, dims, jnp.float32) * deviation
    return jnp.minimum(jnp.maximum(result, -most), most).astype(kind)


def setup_inputs(seed: int = 0) -> dict:
    splits = jax.random.split(jax.random.key(seed), 13)
    return {
        "feat": draw_feat(jax.random.fold_in(splits[12], 71), 0),
        "norm1_gain": jnp.clip(jax.random.uniform(splits[1], (C,), jnp.float32, 0.5, 1.5), 0.5, 1.5),
        "norm1_bias": gaussian(splits[2], (C,), 0.5, 3.0, jnp.float32),
        "conv_weight": gaussian(splits[3], (3, 3, 3, C, C), (27 * C) ** -0.5, 0.0546875),
        "conv_bias": gaussian(splits[4], (C,), 0.5, 3.0, jnp.float32),
        "norm2_gain": jnp.clip(jax.random.uniform(splits[5], (C,), jnp.float32, 0.5, 1.5), 0.5, 1.5),
        "norm2_bias": gaussian(splits[6], (C,), 0.5, 3.0, jnp.float32),
        "w_query": draw_w_query(jax.random.fold_in(splits[12], 71), 0),
        "w_key": draw_w_key(jax.random.fold_in(splits[12], 71), 0),
        "w_value": gaussian(splits[9], (C, C), C ** -0.5, 0.25),
        "w_out": gaussian(splits[10], (C, C), C ** -0.5, 0.25),
        "out_bias": gaussian(splits[11], (C,), 0.5, 3.0, jnp.float32),
    }


EPS = 1e-06

def group_norm(values, gain, shift):
    chans = values.shape[-1]
    grouped = values.reshape(values.shape[:-1] + (GROUPS, chans // GROUPS))
    count = values.shape[0] * values.shape[1] * values.shape[2] * (chans // GROUPS)
    mean = lax.optimization_barrier(jnp.sum(grouped, axis=(0, 1, 2, 4))) / count
    centered = grouped - mean[:, None]
    spread = lax.optimization_barrier(jnp.sum(centered * centered, axis=(0, 1, 2, 4))) / count
    normed = centered * lax.rsqrt(spread + EPS)[:, None]
    return normed.reshape(values.shape) * gain + shift

def conv_taps(padded, weight, frames, height, width):
    chans = padded.shape[-1]
    total = jnp.zeros((frames * height * width, weight.shape[-1]), jnp.float32)
    for step_t in range(3):
        for step_h in range(3):
            slab = padded[step_t:step_t + frames, step_h:step_h + height]
            stacked = jnp.concatenate([slab[:, :, step_w:step_w + width] for step_w in range(3)], axis=-1)
            total = total + jnp.dot(stacked.reshape(-1, 3 * chans), weight[step_t, step_h].reshape(3 * chans, -1), preferred_element_type=jnp.float32)
    return total.reshape(frames, height, width, -1)

def attend(query, keys, values, valid):
    scale = 1.0 / math.sqrt(query.shape[-1])
    scores = jnp.einsum('fqc,fkc->fqk', query, keys, preferred_element_type=jnp.float32) * scale
    scores = jnp.where(valid[None, None, :], scores, jnp.float32(-1e+30))
    top = lax.optimization_barrier(jnp.max(scores, axis=-1, keepdims=True))
    expo = jnp.exp(scores - top)
    total = lax.optimization_barrier(jnp.sum(expo, axis=-1, keepdims=True))
    mixed = jnp.einsum('fqk,fkc->fqc', expo.astype(jnp.bfloat16), values, preferred_element_type=jnp.float32)
    return (mixed / total).astype(jnp.bfloat16)

def reference(feat, norm1_gain, norm1_bias, conv_weight, conv_bias, norm2_gain, norm2_bias, w_query, w_key, w_value, w_out, out_bias):
    frames, height, width, chans = feat.shape
    act = jax.nn.silu(group_norm(feat.astype(jnp.float32), norm1_gain, norm1_bias)).astype(jnp.bfloat16)
    timed = jnp.concatenate([act[:1], act[:1], act], axis=0)
    padded = jnp.pad(timed, ((0, 0), (1, 1), (1, 1), (0, 0)))
    conv = conv_taps(padded, conv_weight, frames, height, width) + conv_bias
    resid = (feat.astype(jnp.float32) + conv).astype(jnp.bfloat16)
    normed = group_norm(resid.astype(jnp.float32), norm2_gain, norm2_bias).astype(jnp.bfloat16)
    flat = normed.reshape(-1, chans)
    shape4 = (frames, height, width, chans)
    query = jnp.dot(flat, w_query, preferred_element_type=jnp.float32).astype(jnp.bfloat16).reshape(shape4)
    keys = jnp.dot(flat, w_key, preferred_element_type=jnp.float32).astype(jnp.bfloat16).reshape(shape4)
    values = jnp.dot(flat, w_value, preferred_element_type=jnp.float32).astype(jnp.bfloat16).reshape(shape4)
    reach = RADIUS * ROWS_DEV
    span = 2 * reach + ROWS_DEV
    keys_pad = jnp.pad(keys, ((0, 0), (reach, reach), (0, 0), (0, 0)))
    values_pad = jnp.pad(values, ((0, 0), (reach, reach), (0, 0), (0, 0)))
    offsets = jnp.arange(span, dtype=jnp.int32)

    def stripe(index):
        start = (index * ROWS_DEV).astype(jnp.int32)
        qblock = lax.dynamic_slice_in_dim(query, start, ROWS_DEV, 1).reshape(frames, -1, chans)
        kblock = lax.dynamic_slice_in_dim(keys_pad, start, span, 1).reshape(frames, -1, chans)
        vblock = lax.dynamic_slice_in_dim(values_pad, start, span, 1).reshape(frames, -1, chans)
        place = start - reach + offsets
        valid = jnp.repeat((place >= 0) & (place < height), width)
        return attend(qblock, kblock, vblock, valid)
    blocks = lax.map(stripe, jnp.arange(N_ROWS, dtype=jnp.int32))
    attn = blocks.reshape(N_ROWS, frames, ROWS_DEV, width, chans).transpose(1, 0, 2, 3, 4).reshape(-1, chans)
    mixed = jnp.dot(attn, w_out, preferred_element_type=jnp.float32).reshape(shape4)
    return (resid.astype(jnp.float32) + out_bias + mixed).astype(jnp.bfloat16)
```

```python
import functools
import math

import jax
import jax.numpy as jnp
import numpy as np
from jax import lax
from jax.experimental import pallas as pl
from jax.experimental.pallas import tpu as pltpu
from jax.sharding import Mesh, PartitionSpec as P

GROUPS = 32
EPS = 1e-06
AXES = ("tm", "z", "x", "y")
NZ, NX, NY = 4, 4, 4
LOG2E = 1.4426950408889634
VMEM_LIMIT = 60 * 1024 * 1024
BF = jnp.bfloat16
F32 = jnp.float32


def lin(t, z, x, y):
    return ((t * NZ + z) * NX + x) * NY + y


def pairs_of(move):
    found = []
    for t in range(2):
        for z in range(NZ):
            for x in range(NX):
                for y in range(NY):
                    dest = move(t, z, x, y)
                    if dest is not None:
                        found.append((lin(t, z, x, y), lin(*dest)))
    return found


def send(value, move):
    return lax.ppermute(value, AXES, pairs_of(move))


def rows_by(step):
    def move(t, z, x, y):
        row = (z * NX + x) * NY + y + step
        if 0 <= row < NZ * NX * NY:
            return (t, row // (NX * NY), (row // NY) % NX, row % NY)
        return None

    return move


def blocks_by(step):
    def move(t, z, x, y):
        block = z * NX + x + step
        if 0 <= block < NZ * NX:
            return (t, block // NX, block % NX, y)
        return None

    return move


def turned(axis, step):
    def move(t, z, x, y):
        if axis == "tm":
            return (1 - t, z, x, y)
        if axis == "z":
            return (t, (z + step) % NZ, x, y)
        if axis == "x":
            return (t, z, (x + step) % NX, y)
        return (t, z, x, (y + step) % NY)

    return move


def to_frames(order):
    def move(t, z, x, y):
        return (y // 2, z, x, 2 * t + ((y + order) & 1))

    return move


def to_stripes(order):
    forward = to_frames(order)
    back = {}
    for t in range(2):
        for y in range(NY):
            dest = forward(t, 0, 0, y)
            back[(dest[0], dest[3])] = (t, y)

    def move(t, z, x, y):
        there = back[(t, y)]
        return (there[0], z, x, there[1])

    return move


def merge(parts):
    count = len(parts)
    mean = sum(p[0] for p in parts) / count
    spread = sum(p[1] for p in parts) / count
    away = sum((p[0] - mean) * (p[0] - mean) for p in parts) / count
    return jnp.stack([mean, spread + away])


def global_stats(stats):
    stats = merge([stats, send(stats, turned("tm", 1))])
    for axis in ("z", "x", "y"):
        stats = merge([stats] + [send(stats, turned(axis, k)) for k in (1, 2, 3)])
    return stats


def group_mean(row):
    chans = row.shape[-1]
    size = chans // GROUPS
    lane = lax.broadcasted_iota(jnp.int32, row.shape, 1)
    step = 1
    while step < size:
        low = (lane & step) == 0
        row = row + jnp.where(
            low, pltpu.roll(row, chans - step, 1), pltpu.roll(row, step, 1)
        )
        step *= 2
    return row / size


def local_stats(blocks, stat_ref):
    chans = stat_ref.shape[-1]
    cells = sum(b.shape[0] for b in [f() for f in blocks])
    total = sum(jnp.sum(f().astype(F32), axis=0, keepdims=True) for f in blocks)
    mean = group_mean(jnp.broadcast_to(total / cells, (8, chans)))
    center = mean[0:1]
    square = 0.0
    for f in blocks:
        away = f().astype(F32) - center
        square = square + jnp.sum(away * away, axis=0, keepdims=True)
    spread = group_mean(jnp.broadcast_to(square / cells, (8, chans)))
    stat_ref[0:1, :] = center
    stat_ref[1:2, :] = spread[0:1]


def edge_kernel(feat_ref, stat_ref, top_ref, low_ref):
    frames = feat_ref.shape[0]
    for f in range(frames):
        top_ref[f] = feat_ref[f, 0]
        low_ref[f] = feat_ref[f, 1]
    local_stats(
        [functools.partial(lambda f, h: feat_ref[f, h], f, h) for f in range(frames) for h in range(2)],
        stat_ref,
    )


def affine(stat_ref, gain_ref, bias_ref):
    scale = lax.rsqrt(stat_ref[1:2, :] + EPS) * gain_ref[...]
    return scale, bias_ref[...] - stat_ref[0:1, :] * scale


def conv_kernel(
    flags,
    stat_ref,
    gain_ref,
    bias_ref,
    own_ref,
    up_ref,
    down_ref,
    past_ref,
    past_up_ref,
    past_down_ref,
    weight_ref,
    conv_bias_ref,
    out0_ref,
    out1_ref,
    out_stat_ref,
    act_ref,
    acc_ref,
):
    step = pl.program_id(0)
    width, chans = own_ref.shape[2], own_ref.shape[3]
    later, parity, has_up, has_down = flags[0], flags[1], flags[2], flags[3]

    @pl.when(step == 0)
    def _():
        scale, shift = affine(stat_ref, gain_ref, bias_ref)
        row_id = lax.broadcasted_iota(jnp.int32, (width, chans), 0)

        def put(frame, row, value, keep):
            pre = value.astype(F32) * scale + shift
            act = pre / (1.0 + jnp.exp(-pre))
            if keep is not None:
                act = jnp.where(keep > 0, act, 0.0)
            left = jnp.where(row_id == 0, 0.0, pltpu.roll(act, 1, 0))
            right = jnp.where(row_id == width - 1, 0.0, pltpu.roll(act, width - 1, 0))
            act_ref[frame, row, :, 0:chans] = left.astype(BF)
            act_ref[frame, row, :, chans : 2 * chans] = act.astype(BF)
            act_ref[frame, row, :, 2 * chans : 3 * chans] = right.astype(BF)

        for f in range(2):
            put(2 + f, 0, up_ref[f], has_up)
            put(2 + f, 1, own_ref[f, 0], None)
            put(2 + f, 2, own_ref[f, 1], None)
            put(2 + f, 3, down_ref[f], has_down)

        @pl.when(later == 1)
        def _():
            for f in range(2):
                put(f, 0, past_up_ref[f], has_up)
                put(f, 1, past_ref[f, 0], None)
                put(f, 2, past_ref[f, 1], None)
                put(f, 3, past_down_ref[f], has_down)

        @pl.when(later == 0)
        def _():
            for f in range(2):
                for row in range(4):
                    act_ref[f, row] = act_ref[2, row]

    tap_t, tap_h = step // 3, step % 3
    slab = act_ref[pl.ds(tap_t, 2), pl.ds(tap_h, 2)].reshape(4 * width, 3 * chans)
    part = jnp.dot(slab, weight_ref[0], preferred_element_type=F32)

    @pl.when(step == 0)
    def _():
        acc_ref[...] = part.reshape(acc_ref.shape)

    @pl.when(step > 0)
    def _():
        acc_ref[...] += part.reshape(acc_ref.shape)

    @pl.when(step == 8)
    def _():
        outs = (out0_ref, out1_ref)
        for p in range(2):
            frame = (parity + p) & 1
            for h in range(2):
                value = own_ref[frame, h].astype(F32) + (acc_ref[frame, h] + conv_bias_ref[...])
                outs[p][h * width : (h + 1) * width, :] = value.astype(BF)
        local_stats(
            [
                functools.partial(lambda p, h: outs[p][h * width : (h + 1) * width, :], p, h)
                for p in range(2)
                for h in range(2)
            ],
            out_stat_ref,
        )


KEYS = 4352
PAD = 32
SPLITS = (1280, 1024, 1024, 1024)


def attend_kernel(
    flags,
    stat_ref,
    gain_ref,
    bias_ref,
    own0_ref,
    own1_ref,
    swap0_ref,
    swap1_ref,
    relay0_ref,
    relay1_ref,
    prev0_ref,
    prev1_ref,
    next0_ref,
    next1_ref,
    wq_ref,
    wk_ref,
    wv_ref,
    wo_ref,
    out_bias_ref,
    out0_ref,
    out1_ref,
    key_ref,
    mask_ref,
):
    cells, chans = own0_ref.shape
    low, prev_ok, next_ok, relay_ok = flags[0], flags[1], flags[2], flags[3]
    scale, shift = affine(stat_ref, gain_ref, bias_ref)

    def put(place, ref):
        start = place * cells
        if not isinstance(place, int):
            start = pl.multiple_of(start, 16)
        key_ref[pl.ds(start, cells), :] = (ref[...].astype(F32) * scale + shift).astype(BF)

    high = 1 - low
    put(1, own0_ref)
    put(2, own1_ref)
    put(3, swap0_ref)
    put(4, swap1_ref)
    put(5, relay0_ref)
    put(6, relay1_ref)
    put(7 * low, prev0_ref)
    put(7 * high, prev1_ref)
    put(8 + high, next1_ref)
    put(8 + low, next0_ref)

    place = lax.broadcasted_iota(jnp.int32, (1, KEYS), 1)
    for upper in range(2):
        row = place + upper * (cells - PAD)
        stripe_ok = jnp.where(
            (row < cells) | ((row >= 7 * cells) & (row < 8 * cells)),
            prev_ok,
            jnp.where(row >= 8 * cells, next_ok, jnp.where((row >= 5 * cells) & (row < 7 * cells), relay_ok, 1)),
        )
        inside = (row < 9 * cells) if upper == 0 else (row >= cells)
        mask_ref[upper : upper + 1, :] = jnp.where(inside & (stripe_ok > 0), 0.0, -1e30)

    factor = LOG2E / math.sqrt(chans)
    for p, (own_ref, out_ref) in enumerate(((own0_ref, out0_ref), (own1_ref, out1_ref))):
        upper = low ^ p
        normed = key_ref[(1 + p) * cells : (2 + p) * cells, :]
        query = jnp.dot(normed, wq_ref[...], preferred_element_type=F32).astype(BF)
        query = lax.dot_general(
            query, wk_ref[...], (((1,), (1,)), ((), ())), preferred_element_type=F32
        )
        query = (query * factor).astype(BF)
        top = jnp.full((cells, 1), -jnp.inf, F32)
        total = jnp.zeros((cells, 1), F32)
        acc = jnp.zeros((cells, chans), F32)
        start = 0
        for size in SPLITS:
            begin = pl.multiple_of(upper * (cells - PAD) + start, 16)
            block = key_ref[pl.ds(begin, size), :]
            score = lax.dot_general(
                query, block, (((1,), (1,)), ((), ())), preferred_element_type=F32
            )
            score = score + mask_ref[pl.ds(upper, 1), start : start + size]
            new_top = jnp.maximum(top, jnp.max(score, axis=-1, keepdims=True))
            weight = jnp.exp2(score - new_top)
            fade = jnp.exp2(top - new_top)
            total = total * fade + jnp.sum(weight, axis=-1, keepdims=True)
            acc = acc * fade + jnp.dot(weight.astype(BF), block, preferred_element_type=F32)
            top = new_top
            start += size
        mixed = (acc / total).astype(BF)
        attn = jnp.dot(mixed, wv_ref[...], preferred_element_type=F32).astype(BF)
        result = jnp.dot(attn, wo_ref[...], preferred_element_type=F32)
        out_ref[...] = (own_ref[...].astype(F32) + out_bias_ref[...] + result).astype(BF)


def whole():
    return pl.BlockSpec(memory_space=pltpu.VMEM)


def flag_spec():
    return pl.BlockSpec(memory_space=pltpu.SMEM)


def params():
    return pltpu.CompilerParams(vmem_limit_bytes=VMEM_LIMIT)


def shards(
    feat,
    norm1_gain,
    norm1_bias,
    conv_weight,
    conv_bias,
    norm2_gain,
    norm2_bias,
    w_query,
    w_key,
    w_value,
    w_out,
    out_bias,
):
    frames, rows, width, chans = feat.shape
    t, z, x, y = (lax.axis_index(a) for a in AXES)
    block = z * NX + x
    stripe = block * NY + y
    i32 = lambda *v: jnp.stack([jnp.asarray(a, jnp.int32) for a in v])
    line = lambda v: v.reshape(1, chans)

    edge = jax.ShapeDtypeStruct((frames, width, chans), BF)
    stat_shape = jax.ShapeDtypeStruct((2, chans), F32)
    stats, top, low = pl.pallas_call(
        edge_kernel,
        out_shape=(stat_shape, edge, edge),
        in_specs=[whole()],
        out_specs=(whole(), whole(), whole()),
        compiler_params=params(),
        name="edges",
    )(feat)
    up = send(low, rows_by(1))
    down = send(top, rows_by(-1))
    past = send(feat, turned("tm", 1))
    past_up = send(up, turned("tm", 1))
    past_down = send(down, turned("tm", 1))
    stats = global_stats(stats)

    flags = i32(t, y & 1, stripe > 0, stripe < NZ * NX * NY - 1)
    full = lambda a: pl.BlockSpec(a.shape, lambda i, *_: (0,) * a.ndim)
    cells = rows * width
    piece = jax.ShapeDtypeStruct((cells, chans), BF)
    args = (stats, line(norm1_gain), line(norm1_bias), feat, up, down, past, past_up, past_down)
    own0, own1, stats2 = pl.pallas_call(
        conv_kernel,
        out_shape=(piece, piece, stat_shape),
        grid_spec=pltpu.PrefetchScalarGridSpec(
            num_scalar_prefetch=1,
            grid=(9,),
            in_specs=[full(a) for a in args]
            + [
                pl.BlockSpec((1, 3 * chans, chans), lambda i, *_: (i, 0, 0)),
                pl.BlockSpec((1, chans), lambda i, *_: (0, 0)),
            ],
            out_specs=(full(piece), full(piece), full(stat_shape)),
            scratch_shapes=[
                pltpu.VMEM((4, 4, width, 3 * chans), BF),
                pltpu.VMEM((frames, rows, width, chans), F32),
            ],
        ),
        compiler_params=params(),
        name="conv",
    )(flags, *args, conv_weight.reshape(9, 3 * chans, chans), line(conv_bias))

    mine0 = send(own0, to_frames(0))
    mine1 = send(own1, to_frames(1))
    prev0 = send(mine0, blocks_by(1))
    next0 = send(mine0, blocks_by(-1))
    prev1 = send(mine1, blocks_by(1))
    next1 = send(mine1, blocks_by(-1))
    swap0 = send(mine0, turned("tm", 1))
    swap1 = send(mine1, turned("tm", 1))
    relay0 = send(jnp.where(t == 1, prev0, next0), turned("tm", 1))
    relay1 = send(jnp.where(t == 1, prev1, next1), turned("tm", 1))
    stats2 = global_stats(stats2)

    prev_ok = block > 0
    next_ok = block < NZ * NX - 1
    flags2 = i32(y & 1, prev_ok, next_ok, jnp.where(t == 0, prev_ok, next_ok))
    out0, out1 = pl.pallas_call(
        attend_kernel,
        out_shape=(piece, piece),
        in_specs=[flag_spec()] + [whole()] * 18,
        out_specs=(whole(), whole()),
        scratch_shapes=[
            pltpu.VMEM((10 * cells, chans), BF),
            pltpu.VMEM((2, KEYS), F32),
        ],
        compiler_params=params(),
        name="attend",
    )(
        flags2,
        stats2,
        line(norm2_gain),
        line(norm2_bias),
        mine0,
        mine1,
        swap0,
        swap1,
        relay0,
        relay1,
        prev0,
        prev1,
        next0,
        next1,
        w_query,
        w_key,
        w_value,
        w_out,
        line(out_bias),
    )
    back0 = send(out0, to_stripes(0))
    back1 = send(out1, to_stripes(1))
    odd = (y & 1) == 1
    output = jnp.stack([jnp.where(odd, back1, back0), jnp.where(odd, back0, back1)])
    return output.reshape(feat.shape)


def solution(mesh):
    fine = Mesh(mesh.devices.reshape(2, NZ, NX, NY), AXES)
    place = P("tm", ("z", "x", "y"), None, None)
    return jax.shard_map(
        shards,
        mesh=fine,
        in_specs=(place,) + (P(),) * 11,
        out_specs=place,
        check_vma=False,
    )
```

```python
import functools
import math

import jax
import jax.numpy as jnp
import numpy as np
from jax import lax
from jax.experimental import pallas as pl
from jax.experimental.pallas import tpu as pltpu
from jax.sharding import Mesh, PartitionSpec as P

GROUPS = 32
EPS = 1e-06
AXES = ("tm", "z", "x", "y")
NZ, NX, NY = 4, 4, 4
LOG2E = 1.4426950408889634
CONV = 40
OWN = 24
TAIL = 24
BF = jnp.bfloat16
F32 = jnp.float32


def lin(t, z, x, y):
    return ((t * NZ + z) * NX + x) * NY + y


def pairs_of(move):
    found = []
    for t in range(2):
        for z in range(NZ):
            for x in range(NX):
                for y in range(NY):
                    dest = move(t, z, x, y)
                    if dest is not None:
                        found.append((lin(t, z, x, y), lin(*dest)))
    return found


def send(value, move):
    return lax.ppermute(value, AXES, pairs_of(move))


def edges_out(t, z, x, y):
    row = (z * NX + x) * NY + y + (1 - 2 * t)
    if 0 <= row < NZ * NX * NY:
        return (t, row // (NX * NY), (row // NY) % NX, row % NY)
    return None


def blocks_out(t, z, x, y):
    block = z * NX + x + (1 - 2 * t)
    if 0 <= block < NZ * NX:
        return (t, block // NX, block % NX, y)
    return None


def turned(axis, step):
    def move(t, z, x, y):
        if axis == "tm":
            return (1 - t, z, x, y)
        if axis == "z":
            return (t, (z + step) % NZ, x, y)
        if axis == "x":
            return (t, z, (x + step) % NX, y)
        return (t, z, x, (y + step) % NY)

    return move


def to_frames(order):
    def move(t, z, x, y):
        return (y // 2, z, x, 2 * t + ((y + order) & 1))

    return move


def to_stripes(order):
    forward = to_frames(order)
    back = {}
    for t in range(2):
        for y in range(NY):
            dest = forward(t, 0, 0, y)
            back[(dest[0], dest[3])] = (t, y)

    def move(t, z, x, y):
        there = back[(t, y)]
        return (there[0], z, x, there[1])

    return move


def merge(parts):
    count = len(parts)
    mid = sum(parts) / count
    away = [p[0:1] - mid[0:1] for p in parts]
    extra = sum(a * a for a in away) / count
    row = lax.broadcasted_iota(jnp.int32, mid.shape, 0)
    return mid + jnp.where(row == 1, jnp.broadcast_to(extra, mid.shape), 0.0)


def gathered(stats, axis):
    steps = (1,) if axis == "tm" else (1, 2, 3)
    return [stats] + [send(stats, turned(axis, k)) for k in steps]


def over(stats, axis):
    return merge(gathered(stats, axis))


def after(value, *first):
    return lax.optimization_barrier((value,) + first)[0]


def group_mean(row):
    chans = row.shape[-1]
    size = chans // GROUPS
    lane = lax.broadcasted_iota(jnp.int32, row.shape, 1)
    step = 1
    while step < size:
        low = (lane & step) == 0
        row = row + jnp.where(
            low, pltpu.roll(row, chans - step, 1), pltpu.roll(row, step, 1)
        )
        step *= 2
    return row / size


def local_stats(blocks, stat_ref):
    chans = stat_ref.shape[-1]
    cells = sum(b.shape[0] for b in [f() for f in blocks])
    total = sum(jnp.sum(f().astype(F32), axis=0, keepdims=True) for f in blocks)
    mean = group_mean(jnp.broadcast_to(total / cells, (8, chans)))
    center = mean[0:1]
    square = 0.0
    for f in blocks:
        away = f().astype(F32) - center
        square = square + jnp.sum(away * away, axis=0, keepdims=True)
    spread = group_mean(jnp.broadcast_to(square / cells, (8, chans)))
    stat_ref[0:1, :] = center
    stat_ref[1:2, :] = spread[0:1]


def edge_kernel(flags, feat_ref, other_ref, stat_ref, edge_ref):
    frames = feat_ref.shape[0]
    core = flags[0]
    row = 1 - core
    for f in range(frames):
        edge_ref[frames * core + f] = feat_ref[f, row]
        edge_ref[frames * (1 - core) + f] = other_ref[f, row]
    local_stats(
        [
            functools.partial(lambda ref, f, h: ref[f, h], ref, f, h)
            for ref in (feat_ref, other_ref)
            for f in range(frames)
            for h in range(2)
        ],
        stat_ref,
    )


def affine(stat_ref, gain_ref, bias_ref):
    scale = lax.rsqrt(stat_ref[1:2, :] + EPS) * gain_ref[...]
    return scale, bias_ref[...] - stat_ref[0:1, :] * scale


def conv_kernel(
    flags,
    stat_ref,
    gain_ref,
    bias_ref,
    own_ref,
    past_ref,
    edge_ref,
    cross_ref,
    weight_ref,
    conv_bias_ref,
    out0_ref,
    out1_ref,
    act_ref,
    acc_ref,
    tap_ref,
    sems,
):
    width, chans = own_ref.shape[2], own_ref.shape[3]
    later, parity = flags[0] == 1, flags[1]
    keep = {0: jnp.where(flags[2] > 0, 1.0, 0.0), 3: jnp.where(flags[3] > 0, 1.0, 0.0)}
    copies = [
        pltpu.make_async_copy(weight_ref.at[i], tap_ref.at[i], sems.at[i]) for i in range(9)
    ]
    for copy in copies:
        copy.start()
    scale, shift = affine(stat_ref, gain_ref, bias_ref)
    half_scale, half_shift = scale * 0.5, shift * 0.5
    zero = jnp.zeros((1, chans), BF)

    def put(frame, row):
        if row in keep:
            at = jnp.maximum(2 * flags[0] - 2 + frame, 0)
            mine, theirs = edge_ref[at], cross_ref[at]
            raw = jnp.where(later, theirs, mine) if row == 0 else jnp.where(later, mine, theirs)
        elif frame >= 2:
            raw = own_ref[frame - 2, row - 1]
        else:
            raw = jnp.where(later, past_ref[frame, row - 1], own_ref[0, row - 1])
        raw = raw.astype(F32)
        half = raw * half_scale + half_shift
        act = half + half * jnp.tanh(half)
        if row in keep:
            act = act * keep[row]
        act = act.astype(BF)
        act_ref[frame, row, :, 0:chans] = jnp.concatenate([zero, act[: width - 1]], axis=0)
        act_ref[frame, row, :, chans : 2 * chans] = act
        act_ref[frame, row, :, 2 * chans : 3 * chans] = jnp.concatenate([act[1:], zero], axis=0)

    ready = set()
    for i in range(9):
        tap_t, tap_h = i // 3, i % 3
        for frame in (tap_t, tap_t + 1):
            for row in (tap_h, tap_h + 1):
                if (frame, row) not in ready:
                    ready.add((frame, row))
                    put(frame, row)
        copies[i].wait()
        slab = act_ref[tap_t : tap_t + 2, tap_h : tap_h + 2].reshape(4 * width, 3 * chans)
        part = jnp.dot(slab, tap_ref[i], preferred_element_type=F32).reshape(acc_ref.shape)
        if i == 0:
            acc_ref[...] = part
        else:
            acc_ref[...] += part

    outs = (out0_ref, out1_ref)
    for p in range(2):
        frame = (parity + p) & 1
        for h in range(2):
            value = own_ref[frame, h].astype(F32) + (acc_ref[frame, h] + conv_bias_ref[...])
            outs[p][h * width : (h + 1) * width, :] = value.astype(BF)


def stat_kernel(first_ref, second_ref, stat_ref):
    half = first_ref.shape[0] // 2
    local_stats(
        [
            functools.partial(lambda ref, h: ref[h * half : (h + 1) * half, :], ref, h)
            for ref in (first_ref, second_ref)
            for h in range(2)
        ],
        stat_ref,
    )


def dot_t(a, b):
    return lax.dot_general(a, b, (((1,), (1,)), ((), ())), preferred_element_type=F32)


def gather(query, block, mask, state):
    score = dot_t(query, block)
    if mask is not None:
        score = score + mask
    top = jnp.max(score, axis=-1, keepdims=True)
    if state is not None:
        top = jnp.maximum(state[0], top)
    weight = jnp.exp2(score - top)
    total = jnp.sum(weight, axis=-1, keepdims=True)
    acc = jnp.dot(weight.astype(BF), block, preferred_element_type=F32)
    if state is not None:
        fade = jnp.exp2(state[0] - top)
        total = state[1] * fade + total
        acc = state[2] * fade + acc
    return top, total, acc


def keep_state(state, acc_ref, sum_ref):
    top, total, acc = state
    acc_ref[...] = acc
    lane = lax.broadcasted_iota(jnp.int32, sum_ref.shape, 1)
    sum_ref[...] = jnp.where(lane == 0, top, total)


def load_state(acc_ref, sum_ref):
    return sum_ref[:, 0:1], sum_ref[:, 1:2], acc_ref[...]


def reach_mask(flags, order, far_side, row, start, cells):
    core, low = flags[0], flags[1]
    side = core ^ far_side
    fine = jnp.where(side == 0, flags[4], flags[5])
    mask = 0.0
    for p in range(2):
        key_upper, query_upper = low ^ p, low ^ order
        seen = jnp.where(side == 0, key_upper >= query_upper, key_upper <= query_upper)
        here = (row >= start + p * cells) & (row < start + (p + 1) * cells)
        mask = mask + jnp.where(here & jnp.logical_not(seen & (fine > 0)), -1e30, 0.0)
    return mask


OWN_KEYS = 2944


def own_kernel(
    flags,
    stat_ref,
    gain_ref,
    bias_ref,
    mine_ref,
    swap_ref,
    near_ref,
    wq_ref,
    wk_ref,
    query0_ref,
    query1_ref,
    acc0_ref,
    acc1_ref,
    sum0_ref,
    sum1_ref,
    key_ref,
):
    cells, chans = query0_ref.shape
    scale, shift = affine(stat_ref, gain_ref, bias_ref)
    for i, ref in enumerate((mine_ref, swap_ref, near_ref)):
        raw = ref[...].astype(F32)
        key_ref[2 * i * cells : 2 * (i + 1) * cells, :] = (raw * scale + shift).astype(BF)
    key_ref[6 * cells : OWN_KEYS, :] = jnp.zeros((OWN_KEYS - 6 * cells, chans), BF)
    factor = LOG2E / math.sqrt(chans)
    queries = (query0_ref, query1_ref)
    for p in range(2):
        normed = key_ref[p * cells : (p + 1) * cells, :]
        query = jnp.dot(normed, wq_ref[...], preferred_element_type=F32).astype(BF)
        queries[p][...] = (dot_t(query, wk_ref[...]) * factor).astype(BF)
    row = lax.broadcasted_iota(jnp.int32, (1, OWN_KEYS), 1)
    for p, (acc_ref, sum_ref) in enumerate(((acc0_ref, sum0_ref), (acc1_ref, sum1_ref))):
        mask = reach_mask(flags, p, 0, row, 4 * cells, cells)
        mask = mask + jnp.where(row >= 6 * cells, -1e30, 0.0)
        keep_state(gather(queries[p][...], key_ref[...], mask, None), acc_ref, sum_ref)


def tail_kernel(
    order,
    flags,
    stat_ref,
    gain_ref,
    bias_ref,
    far_ref,
    relay_ref,
    query_ref,
    acc_ref,
    sum_ref,
    own_ref,
    wv_ref,
    wo_ref,
    out_bias_ref,
    out_ref,
    key_ref,
):
    cells = out_ref.shape[0]
    scale, shift = affine(stat_ref, gain_ref, bias_ref)
    for i, ref in enumerate((far_ref, relay_ref)):
        raw = ref[...].astype(F32)
        key_ref[2 * i * cells : 2 * (i + 1) * cells, :] = (raw * scale + shift).astype(BF)
    row = lax.broadcasted_iota(jnp.int32, (1, 4 * cells), 1)
    mask = reach_mask(flags, order, 1, row, 2 * cells, cells)
    far_ok = jnp.where(flags[0] == 0, flags[4], flags[5])
    mask = mask + jnp.where((row < 2 * cells) & (far_ok == 0), -1e30, 0.0)
    state = load_state(acc_ref, sum_ref)
    _, total, acc = gather(query_ref[...], key_ref[...], mask, state)
    mixed = (acc / total).astype(BF)
    attn = jnp.dot(mixed, wv_ref[...], preferred_element_type=F32).astype(BF)
    result = jnp.dot(attn, wo_ref[...], preferred_element_type=F32)
    own = own_ref[...].astype(F32)
    out_ref[...] = (own + out_bias_ref[...] + result).astype(BF)


def place_kernel(flags, back0_ref, back1_ref, out_ref):
    odd = flags[1]
    out_ref[odd] = back0_ref[...]
    out_ref[1 - odd] = back1_ref[...]


def whole():
    return pl.BlockSpec(memory_space=pltpu.VMEM)


def remote():
    return pl.BlockSpec(memory_space=pl.ANY)


def cost(flops, moved):
    return pl.CostEstimate(flops=int(flops), bytes_accessed=int(moved), transcendentals=0)


def flag_spec():
    return pl.BlockSpec(memory_space=pltpu.SMEM)


def params(mib):
    return pltpu.CompilerParams(vmem_limit_bytes=mib * 1024 * 1024)


def shards(
    feat,
    norm1_gain,
    norm1_bias,
    conv_weight,
    conv_bias,
    norm2_gain,
    norm2_bias,
    w_query,
    w_key,
    w_value,
    w_out,
    out_bias,
):
    frames, rows, width, chans = feat.shape
    t, z, x, y = (lax.axis_index(a) for a in AXES)
    block = z * NX + x
    stripe = block * NY + y
    i32 = lambda *v: jnp.stack([jnp.asarray(a, jnp.int32) for a in v])
    line = lambda v: v.reshape(1, chans)

    stat_shape = jax.ShapeDtypeStruct((2, chans), F32)
    flags = i32(t, y & 1, stripe > 0, stripe < NZ * NX * NY - 1, block > 0, block < NZ * NX - 1)
    swap = turned("tm", 1)
    other = send(feat, swap)
    stats, edge = pl.pallas_call(
        edge_kernel,
        out_shape=(stat_shape, jax.ShapeDtypeStruct((2 * frames, width, chans), BF)),
        in_specs=[flag_spec(), whole(), whole()],
        out_specs=(whole(), whole()),
        compiler_params=params(16),
        name="edges",
    )(flags, feat, other)
    parts = gathered(stats, "y")
    edge = send(after(edge, parts[1]), edges_out)
    stats = over(over(merge(parts), "z"), "x")
    cross = send(after(edge, stats), swap)

    cells = rows * width
    piece = jax.ShapeDtypeStruct((cells, chans), BF)
    own0, own1 = pl.pallas_call(
        conv_kernel,
        out_shape=(piece, piece),
        in_specs=[flag_spec()] + [whole()] * 7 + [remote(), whole()],
        out_specs=(whole(),) * 2,
        scratch_shapes=[
            pltpu.VMEM((4, 4, width, 3 * chans), BF),
            pltpu.VMEM((frames, rows, width, chans), F32),
            pltpu.VMEM((9, 3 * chans, chans), BF),
            pltpu.SemaphoreType.DMA((9,)),
        ],
        compiler_params=params(CONV),
        cost_estimate=cost(27 * 2 * 960 * chans * chans, 20e6),
        name="conv",
    )(
        flags,
        stats,
        line(norm1_gain),
        line(norm1_bias),
        feat,
        other,
        edge,
        cross,
        conv_weight.reshape(9, 3 * chans, chans),
        line(conv_bias),
    )

    mine0 = send(own0, to_frames(0))
    mine1 = send(own1, to_frames(1))
    stats2 = pl.pallas_call(
        stat_kernel,
        out_shape=stat_shape,
        in_specs=[whole(), whole()],
        out_specs=whole(),
        compiler_params=params(16),
        cost_estimate=cost(8e9, 2e6),
        name="stats",
    )(own0, own1)
    stats2 = over(over(stats2, "tm"), "z")
    mine = jnp.concatenate([mine0, mine1])
    swapped = send(mine, swap)
    near = send(after(mine, stats2), blocks_out)
    stats2 = over(stats2, "x")
    far = send(after(swapped, stats2), blocks_out)
    stats2 = over(stats2, "y")

    norm2 = (stats2, line(norm2_gain), line(norm2_bias))
    acc_shape = jax.ShapeDtypeStruct((cells, chans), F32)
    sum_shape = jax.ShapeDtypeStruct((cells, 128), F32)
    query0, query1, acc0, acc1, sum0, sum1 = pl.pallas_call(
        own_kernel,
        out_shape=(piece, piece, acc_shape, acc_shape, sum_shape, sum_shape),
        in_specs=[flag_spec()] + [whole()] * 8,
        out_specs=(whole(),) * 6,
        scratch_shapes=[pltpu.VMEM((OWN_KEYS, chans), BF)],
        compiler_params=params(OWN),
        cost_estimate=cost(6e9, 8e6),
        name="own",
    )(flags, *norm2, mine, swapped, near, w_query, w_key)
    relay = send(after(far, sum1), swap)

    def tail(order, query, acc, total, own):
        return pl.pallas_call(
            functools.partial(tail_kernel, order),
            out_shape=piece,
            in_specs=[flag_spec()] + [whole()] * 12,
            out_specs=whole(),
            scratch_shapes=[pltpu.VMEM((4 * cells, chans), BF)],
            compiler_params=params(TAIL),
            cost_estimate=cost(3e9, 5e6),
            name="tail%d" % order,
        )(
            flags,
            *norm2,
            far,
            relay,
            query,
            acc,
            total,
            own,
            w_value,
            w_out,
            line(out_bias),
        )

    out0 = tail(0, query0, acc0, sum0, mine0)
    out1 = tail(1, query1, acc1, sum1, mine1)
    back0 = send(out0, to_stripes(0))
    back1 = send(out1, to_stripes(1))
    output = pl.pallas_call(
        place_kernel,
        out_shape=jax.ShapeDtypeStruct((frames, cells, chans), BF),
        in_specs=[flag_spec(), whole(), whole()],
        out_specs=whole(),
        name="place",
    )(flags, back0, back1)
    return output.reshape(feat.shape)


def solution(mesh):
    fine = Mesh(mesh.devices.reshape(2, NZ, NX, NY), AXES)
    place = P("tm", ("z", "x", "y"), None, None)
    return jax.shard_map(
        shards,
        mesh=fine,
        in_specs=(place,) + (P(),) * 11,
        out_specs=place,
        check_vma=False,
    )
```

```python
import functools
import math

import jax
import jax.numpy as jnp
import numpy as np
from jax import lax
from jax.experimental import pallas as pl
from jax.experimental.pallas import tpu as pltpu
from jax.sharding import Mesh, PartitionSpec as P

GROUPS = 32
EPS = 1e-06
AXES = ("tm", "z", "x", "y")
NZ, NX, NY = 4, 4, 4
LOG2E = 1.4426950408889634
CONV = 40
OWN = 24
TAIL = 24
BF = jnp.bfloat16
F32 = jnp.float32


def lin(t, z, x, y):
    return ((t * NZ + z) * NX + x) * NY + y


def pairs_of(move):
    found = []
    for t in range(2):
        for z in range(NZ):
            for x in range(NX):
                for y in range(NY):
                    dest = move(t, z, x, y)
                    if dest is not None:
                        found.append((lin(t, z, x, y), lin(*dest)))
    return found


def send(value, move):
    return lax.ppermute(value, AXES, pairs_of(move))


def edges_out(t, z, x, y):
    row = (z * NX + x) * NY + y + (1 - 2 * t)
    if 0 <= row < NZ * NX * NY:
        return (t, row // (NX * NY), (row // NY) % NX, row % NY)
    return None


def blocks_out(t, z, x, y):
    block = z * NX + x + (1 - 2 * t)
    if 0 <= block < NZ * NX:
        return (t, block // NX, block % NX, y)
    return None


def turned(axis, step):
    def move(t, z, x, y):
        if axis == "tm":
            return (1 - t, z, x, y)
        if axis == "z":
            return (t, (z + step) % NZ, x, y)
        if axis == "x":
            return (t, z, (x + step) % NX, y)
        return (t, z, x, (y + step) % NY)

    return move


def to_frames(order):
    def move(t, z, x, y):
        return (y // 2, z, x, 2 * t + ((y + order) & 1))

    return move


def to_stripes(order):
    forward = to_frames(order)
    back = {}
    for t in range(2):
        for y in range(NY):
            dest = forward(t, 0, 0, y)
            back[(dest[0], dest[3])] = (t, y)

    def move(t, z, x, y):
        there = back[(t, y)]
        return (there[0], z, x, there[1])

    return move


def merge(parts):
    count = len(parts)
    mid = sum(parts) / count
    away = [p[0:1] - mid[0:1] for p in parts]
    extra = sum(a * a for a in away) / count
    row = lax.broadcasted_iota(jnp.int32, mid.shape, 0)
    return mid + jnp.where(row == 1, jnp.broadcast_to(extra, mid.shape), 0.0)


def gathered(stats, axis):
    steps = (1,) if axis == "tm" else (1, 2, 3)
    return [stats] + [send(stats, turned(axis, k)) for k in steps]


def over(stats, axis):
    return merge(gathered(stats, axis))


def after(value, *first):
    return lax.optimization_barrier((value,) + first)[0]


def group_mean(row):
    chans = row.shape[-1]
    size = chans // GROUPS
    lane = lax.broadcasted_iota(jnp.int32, row.shape, 1)
    step = 1
    while step < size:
        low = (lane & step) == 0
        row = row + jnp.where(
            low, pltpu.roll(row, chans - step, 1), pltpu.roll(row, step, 1)
        )
        step *= 2
    return row / size


def local_stats(blocks, stat_ref):
    chans = stat_ref.shape[-1]
    cells = sum(b.shape[0] for b in [f() for f in blocks])
    total = sum(jnp.sum(f().astype(F32), axis=0, keepdims=True) for f in blocks)
    mean = group_mean(jnp.broadcast_to(total / cells, (8, chans)))
    center = mean[0:1]
    square = 0.0
    for f in blocks:
        away = f().astype(F32) - center
        square = square + jnp.sum(away * away, axis=0, keepdims=True)
    spread = group_mean(jnp.broadcast_to(square / cells, (8, chans)))
    stat_ref[0:1, :] = center
    stat_ref[1:2, :] = spread[0:1]


def stat_kernel(flags, *refs):
    local_stats(
        [functools.partial(lambda ref, i: ref[i], ref, i) for ref in refs[:-1] for i in range(ref.shape[0])],
        refs[-1],
    )


def edge_kernel(flags, feat_ref, other_ref, first_ref, stat_ref, edge_ref):
    frames = feat_ref.shape[0] // 2
    core = flags[0]
    row = 1 - core
    for f in range(frames):
        edge_ref[frames * core + f] = feat_ref[2 * f + row]
        edge_ref[frames * (1 - core) + f] = other_ref[2 * f + row]
    stat_kernel(flags, other_ref, stat_ref)
    mean, spread = stat_ref[0:1, :], stat_ref[1:2, :]
    away = (mean - first_ref[0:1, :]) * 0.5
    stat_ref[0:1, :] = (mean + first_ref[0:1, :]) * 0.5
    stat_ref[1:2, :] = (spread + first_ref[1:2, :]) * 0.5 + away * away


def affine(stat_ref, vector_ref, first):
    scale = lax.rsqrt(stat_ref[1:2, :] + EPS) * vector_ref[first : first + 1, :]
    return scale, vector_ref[first + 1 : first + 2, :] - stat_ref[0:1, :] * scale


def conv_kernel(
    flags,
    stat_ref,
    vector_ref,
    own_ref,
    past_ref,
    edge_ref,
    cross_ref,
    weight_ref,
    out0_ref,
    out1_ref,
    act_ref,
    acc_ref,
    tap_ref,
    sems,
):
    width, chans = own_ref.shape[2], own_ref.shape[3]
    later, parity = flags[0] == 1, flags[1]
    keep = {0: jnp.where(flags[2] > 0, 1.0, 0.0), 3: jnp.where(flags[3] > 0, 1.0, 0.0)}
    copies = [
        pltpu.make_async_copy(weight_ref.at[i], tap_ref.at[i], sems.at[i]) for i in range(9)
    ]
    for copy in copies:
        copy.start()
    scale, shift = affine(stat_ref, vector_ref, 0)
    half_scale, half_shift = scale * 0.5, shift * 0.5
    zero = jnp.zeros((1, chans), BF)

    def put(frame, row):
        if row in keep:
            at = jnp.maximum(2 * flags[0] - 2 + frame, 0)
            mine, theirs = edge_ref[at], cross_ref[at]
            raw = jnp.where(later, theirs, mine) if row == 0 else jnp.where(later, mine, theirs)
        elif frame >= 2:
            raw = own_ref[frame - 2, row - 1]
        else:
            raw = jnp.where(later, past_ref[frame, row - 1], own_ref[0, row - 1])
        raw = raw.astype(F32)
        half = raw * half_scale + half_shift
        act = half + half * jnp.tanh(half)
        if row in keep:
            act = act * keep[row]
        act = act.astype(BF)
        act_ref[frame, row, :, 0:chans] = jnp.concatenate([zero, act[: width - 1]], axis=0)
        act_ref[frame, row, :, chans : 2 * chans] = act
        act_ref[frame, row, :, 2 * chans : 3 * chans] = jnp.concatenate([act[1:], zero], axis=0)

    ready = set()
    for i in range(9):
        tap_t, tap_h = i // 3, i % 3
        for frame in (tap_t, tap_t + 1):
            for row in (tap_h, tap_h + 1):
                if (frame, row) not in ready:
                    ready.add((frame, row))
                    put(frame, row)
        copies[i].wait()
        slab = act_ref[tap_t : tap_t + 2, tap_h : tap_h + 2].reshape(4 * width, 3 * chans)
        part = jnp.dot(slab, tap_ref[i], preferred_element_type=F32).reshape(acc_ref.shape)
        if i == 0:
            acc_ref[...] = part
        else:
            acc_ref[...] += part

    outs = (out0_ref, out1_ref)
    for p in range(2):
        frame = (parity + p) & 1
        for h in range(2):
            value = own_ref[frame, h].astype(F32) + (acc_ref[frame, h] + vector_ref[2:3, :])
            outs[p][h * width : (h + 1) * width, :] = value.astype(BF)


def dot_t(a, b):
    return lax.dot_general(a, b, (((1,), (1,)), ((), ())), preferred_element_type=F32)


def gather(query, block, mask, state):
    score = dot_t(query, block)
    if mask is not None:
        score = score + mask
    top = jnp.max(score, axis=-1, keepdims=True)
    if state is not None:
        top = jnp.maximum(state[0], top)
    weight = jnp.exp2(score - top)
    total = jnp.sum(weight, axis=-1, keepdims=True)
    acc = jnp.dot(weight.astype(BF), block, preferred_element_type=F32)
    if state is not None:
        fade = jnp.exp2(state[0] - top)
        total = state[1] * fade + total
        acc = state[2] * fade + acc
    return top, total, acc


def keep_state(state, acc_ref, sum_ref):
    top, total, acc = state
    acc_ref[...] = acc
    lane = lax.broadcasted_iota(jnp.int32, sum_ref.shape, 1)
    sum_ref[...] = jnp.where(lane == 0, top, total)


def load_state(acc_ref, sum_ref):
    return sum_ref[:, 0:1], sum_ref[:, 1:2], acc_ref[...]


def reach_mask(flags, order, far_side, row, start, cells):
    core, low = flags[0], flags[1]
    side = core ^ far_side
    fine = jnp.where(side == 0, flags[4], flags[5])
    mask = 0.0
    for p in range(2):
        key_upper, query_upper = low ^ p, low ^ order
        seen = jnp.where(side == 0, key_upper >= query_upper, key_upper <= query_upper)
        here = (row >= start + p * cells) & (row < start + (p + 1) * cells)
        mask = mask + jnp.where(here & jnp.logical_not(seen & (fine > 0)), -1e30, 0.0)
    return mask


OWN_KEYS = 2944


def own_kernel(
    flags,
    stat_ref,
    vector_ref,
    mine_ref,
    swap_ref,
    near_ref,
    wq_ref,
    wk_ref,
    query0_ref,
    query1_ref,
    acc0_ref,
    acc1_ref,
    sum0_ref,
    sum1_ref,
    key_ref,
):
    cells, chans = query0_ref.shape
    scale, shift = affine(stat_ref, vector_ref, 3)
    for i, ref in enumerate((mine_ref, swap_ref, near_ref)):
        raw = ref[...].astype(F32)
        key_ref[2 * i * cells : 2 * (i + 1) * cells, :] = (raw * scale + shift).astype(BF)
    key_ref[6 * cells : OWN_KEYS, :] = jnp.zeros((OWN_KEYS - 6 * cells, chans), BF)
    factor = LOG2E / math.sqrt(chans)
    queries = (query0_ref, query1_ref)
    for p in range(2):
        normed = key_ref[p * cells : (p + 1) * cells, :]
        query = jnp.dot(normed, wq_ref[...], preferred_element_type=F32).astype(BF)
        queries[p][...] = (dot_t(query, wk_ref[...]) * factor).astype(BF)
    row = lax.broadcasted_iota(jnp.int32, (1, OWN_KEYS), 1)
    for p, (acc_ref, sum_ref) in enumerate(((acc0_ref, sum0_ref), (acc1_ref, sum1_ref))):
        mask = reach_mask(flags, p, 0, row, 4 * cells, cells)
        mask = mask + jnp.where(row >= 6 * cells, -1e30, 0.0)
        keep_state(gather(queries[p][...], key_ref[...], mask, None), acc_ref, sum_ref)


def tail_kernel(
    order,
    flags,
    stat_ref,
    vector_ref,
    far_ref,
    relay_ref,
    query_ref,
    acc_ref,
    sum_ref,
    own_ref,
    wv_ref,
    wo_ref,
    out_ref,
    key_ref,
):
    cells = out_ref.shape[0]
    scale, shift = affine(stat_ref, vector_ref, 3)
    for i, ref in enumerate((far_ref, relay_ref)):
        raw = ref[...].astype(F32)
        key_ref[2 * i * cells : 2 * (i + 1) * cells, :] = (raw * scale + shift).astype(BF)
    row = lax.broadcasted_iota(jnp.int32, (1, 4 * cells), 1)
    mask = reach_mask(flags, order, 1, row, 2 * cells, cells)
    far_ok = jnp.where(flags[0] == 0, flags[4], flags[5])
    mask = mask + jnp.where((row < 2 * cells) & (far_ok == 0), -1e30, 0.0)
    state = load_state(acc_ref, sum_ref)
    _, total, acc = gather(query_ref[...], key_ref[...], mask, state)
    mixed = (acc / total).astype(BF)
    attn = jnp.dot(mixed, wv_ref[...], preferred_element_type=F32).astype(BF)
    result = jnp.dot(attn, wo_ref[...], preferred_element_type=F32)
    own = own_ref[...].astype(F32)
    out_ref[...] = (own + vector_ref[5:6, :] + result).astype(BF)


def place_kernel(flags, back0_ref, back1_ref, out_ref):
    odd = flags[1]
    out_ref[odd] = back0_ref[...]
    out_ref[1 - odd] = back1_ref[...]


def whole():
    return pl.BlockSpec(memory_space=pltpu.VMEM)


def remote():
    return pl.BlockSpec(memory_space=pl.ANY)


def cost(flops, moved):
    return pl.CostEstimate(flops=int(flops), bytes_accessed=int(moved), transcendentals=0)


def flag_spec():
    return pl.BlockSpec(memory_space=pltpu.SMEM)


def params(mib):
    return pltpu.CompilerParams(vmem_limit_bytes=mib * 1024 * 1024)


def shards(
    feat,
    norm1_gain,
    norm1_bias,
    conv_weight,
    conv_bias,
    norm2_gain,
    norm2_bias,
    w_query,
    w_key,
    w_value,
    w_out,
    out_bias,
):
    frames, rows, width, chans = feat.shape
    t, z, x, y = (lax.axis_index(a) for a in AXES)
    block = z * NX + x
    stripe = block * NY + y
    i32 = lambda *v: jnp.stack([jnp.asarray(a, jnp.int32) for a in v])

    stat_shape = jax.ShapeDtypeStruct((2, chans), F32)
    flags = i32(t, y & 1, stripe > 0, stripe < NZ * NX * NY - 1, block > 0, block < NZ * NX - 1)
    vectors = jnp.stack([norm1_gain, norm1_bias, conv_bias, norm2_gain, norm2_bias, out_bias])
    swap = turned("tm", 1)
    stat_shape = jax.ShapeDtypeStruct((2, chans), F32)

    def stats_of(*pieces):
        return pl.pallas_call(
            stat_kernel,
            out_shape=stat_shape,
            in_specs=[flag_spec()] + [whole()] * len(pieces),
            out_specs=whole(),
            compiler_params=params(16),
            name="stats",
        )(flags, *[a.reshape(-1, width, chans) for a in pieces])

    other = send(feat, swap)
    stats, edge = pl.pallas_call(
        edge_kernel,
        out_shape=(stat_shape, jax.ShapeDtypeStruct((2 * frames, width, chans), BF)),
        in_specs=[flag_spec(), whole(), whole(), whole()],
        out_specs=(whole(), whole()),
        compiler_params=params(16),
        name="edges",
    )(
        flags,
        feat.reshape(-1, width, chans),
        other.reshape(-1, width, chans),
        stats_of(feat),
    )
    edge = send(edge, edges_out)
    stats = over(stats, "z")
    edge, stats = lax.optimization_barrier((edge, stats))
    cross = send(edge, swap)
    stats = over(over(stats, "x"), "y")

    cells = rows * width
    piece = jax.ShapeDtypeStruct((cells, chans), BF)
    own0, own1 = pl.pallas_call(
        conv_kernel,
        out_shape=(piece, piece),
        in_specs=[flag_spec()] + [whole()] * 6 + [remote()],
        out_specs=(whole(),) * 2,
        scratch_shapes=[
            pltpu.VMEM((4, 4, width, 3 * chans), BF),
            pltpu.VMEM((frames, rows, width, chans), F32),
            pltpu.VMEM((9, 3 * chans, chans), BF),
            pltpu.SemaphoreType.DMA((9,)),
        ],
        compiler_params=params(CONV),
        cost_estimate=cost(27 * 2 * 960 * chans * chans, 20e6),
        name="conv",
    )(
        flags,
        stats,
        vectors,
        feat,
        other,
        edge,
        cross,
        conv_weight.reshape(9, 3 * chans, chans),
    )

    mine0 = send(own0, to_frames(0))
    mine1 = send(own1, to_frames(1))
    stats2 = stats_of(own0, own1)
    stats2 = over(over(stats2, "tm"), "z")
    mine = jnp.concatenate([mine0, mine1])
    swapped = send(mine, swap)
    near = send(after(mine, stats2), blocks_out)
    stats2 = over(stats2, "x")
    far = send(after(swapped, stats2), blocks_out)
    stats2 = over(stats2, "y")

    norm2 = (stats2, vectors)
    acc_shape = jax.ShapeDtypeStruct((cells, chans), F32)
    sum_shape = jax.ShapeDtypeStruct((cells, 128), F32)
    query0, query1, acc0, acc1, sum0, sum1 = pl.pallas_call(
        own_kernel,
        out_shape=(piece, piece, acc_shape, acc_shape, sum_shape, sum_shape),
        in_specs=[flag_spec()] + [whole()] * 7,
        out_specs=(whole(),) * 6,
        scratch_shapes=[pltpu.VMEM((OWN_KEYS, chans), BF)],
        compiler_params=params(OWN),
        cost_estimate=cost(6e9, 8e6),
        name="own",
    )(flags, *norm2, mine, swapped, near, w_query, w_key)
    relay = send(after(far, sum1), swap)

    def tail(order, query, acc, total, own):
        return pl.pallas_call(
            functools.partial(tail_kernel, order),
            out_shape=piece,
            in_specs=[flag_spec()] + [whole()] * 10,
            out_specs=whole(),
            scratch_shapes=[pltpu.VMEM((4 * cells, chans), BF)],
            compiler_params=params(TAIL),
            cost_estimate=cost(3e9, 5e6),
            name="tail%d" % order,
        )(
            flags,
            *norm2,
            far,
            relay,
            query,
            acc,
            total,
            own,
            w_value,
            w_out,
        )

    out0 = tail(0, query0, acc0, sum0, mine0)
    out1 = tail(1, query1, acc1, sum1, mine1)
    back0 = send(out0, to_stripes(0))
    back1 = send(out1, to_stripes(1))
    output = pl.pallas_call(
        place_kernel,
        out_shape=jax.ShapeDtypeStruct((frames, cells, chans), BF),
        in_specs=[flag_spec(), whole(), whole()],
        out_specs=whole(),
        compiler_params=params(8),
        name="place",
    )(flags, back0, back1)
    return output.reshape(feat.shape)


def solution(mesh):
    fine = Mesh(mesh.devices.reshape(2, NZ, NX, NY), AXES)
    place = P("tm", ("z", "x", "y"), None, None)
    return jax.shard_map(
        shards,
        mesh=fine,
        in_specs=(place,) + (P(),) * 11,
        out_specs=place,
        check_vma=False,
    )
```

```python
import functools
import math

import jax
import jax.numpy as jnp
import numpy as np
from jax import lax
from jax.experimental import pallas as pl
from jax.experimental.pallas import tpu as pltpu
from jax.sharding import Mesh, PartitionSpec as P

GROUPS = 32
EPS = 1e-06
AXES = ("tm", "z", "x", "y")
NZ, NX, NY = 4, 4, 4
LOG2E = 1.4426950408889634
CONV = 40
OWN = 24
TAIL = 24
BF = jnp.bfloat16
F32 = jnp.float32


def lin(t, z, x, y):
    return ((t * NZ + z) * NX + x) * NY + y


def pairs_of(move):
    found = []
    for t in range(2):
        for z in range(NZ):
            for x in range(NX):
                for y in range(NY):
                    dest = move(t, z, x, y)
                    if dest is not None:
                        found.append((lin(t, z, x, y), lin(*dest)))
    return found


def send(value, move):
    return lax.ppermute(value, AXES, pairs_of(move))


def edges_out(t, z, x, y):
    row = (z * NX + x) * NY + y + (1 - 2 * t)
    if 0 <= row < NZ * NX * NY:
        return (t, row // (NX * NY), (row // NY) % NX, row % NY)
    return None


def blocks_out(t, z, x, y):
    block = z * NX + x + (1 - 2 * t)
    if 0 <= block < NZ * NX:
        return (t, block // NX, block % NX, y)
    return None


def turned(axis, step):
    def move(t, z, x, y):
        if axis == "tm":
            return (1 - t, z, x, y)
        if axis == "z":
            return (t, (z + step) % NZ, x, y)
        if axis == "x":
            return (t, z, (x + step) % NX, y)
        return (t, z, x, (y + step) % NY)

    return move


def to_frames(order):
    def move(t, z, x, y):
        return (y // 2, z, x, 2 * t + ((y + order) & 1))

    return move


def to_stripes(order):
    forward = to_frames(order)
    back = {}
    for t in range(2):
        for y in range(NY):
            dest = forward(t, 0, 0, y)
            back[(dest[0], dest[3])] = (t, y)

    def move(t, z, x, y):
        there = back[(t, y)]
        return (there[0], z, x, there[1])

    return move


def merge(parts):
    count = len(parts)
    mid = sum(parts) / count
    away = [p[0:1] - mid[0:1] for p in parts]
    extra = sum(a * a for a in away) / count
    row = lax.broadcasted_iota(jnp.int32, mid.shape, 0)
    return mid + jnp.where(row == 1, jnp.broadcast_to(extra, mid.shape), 0.0)


def gathered(stats, axis):
    steps = (1,) if axis == "tm" else (1, 2, 3)
    return [stats] + [send(stats, turned(axis, k)) for k in steps]


def over(stats, axis):
    return merge(gathered(stats, axis))


def after(value, *first):
    return lax.optimization_barrier((value,) + first)[0]


def group_mean(row):
    chans = row.shape[-1]
    size = chans // GROUPS
    lane = lax.broadcasted_iota(jnp.int32, row.shape, 1)
    step = 1
    while step < size:
        low = (lane & step) == 0
        row = row + jnp.where(
            low, pltpu.roll(row, chans - step, 1), pltpu.roll(row, step, 1)
        )
        step *= 2
    return row / size


def local_stats(blocks, stat_ref):
    chans = stat_ref.shape[-1]
    cells = sum(b.shape[0] for b in [f() for f in blocks])
    total = sum(jnp.sum(f().astype(F32), axis=0, keepdims=True) for f in blocks)
    mean = group_mean(jnp.broadcast_to(total / cells, (8, chans)))
    center = mean[0:1]
    square = 0.0
    for f in blocks:
        away = f().astype(F32) - center
        square = square + jnp.sum(away * away, axis=0, keepdims=True)
    spread = group_mean(jnp.broadcast_to(square / cells, (8, chans)))
    stat_ref[0:1, :] = center
    stat_ref[1:2, :] = spread[0:1]


def stat_kernel(flags, *refs):
    local_stats(
        [functools.partial(lambda ref, i: ref[i], ref, i) for ref in refs[:-1] for i in range(ref.shape[0])],
        refs[-1],
    )


def first_kernel(flags, feat_ref, few_ref, stat_ref, kept_ref, vector_ref):
    kept_ref[...] = feat_ref[...]
    vector_ref[...] = few_ref[...]
    stat_kernel(flags, feat_ref, stat_ref)


def edge_kernel(flags, feat_ref, other_ref, first_ref, stat_ref, edge_ref):
    frames = feat_ref.shape[0] // 2
    core = flags[0]
    row = 1 - core
    for f in range(frames):
        edge_ref[frames * core + f] = feat_ref[2 * f + row]
        edge_ref[frames * (1 - core) + f] = other_ref[2 * f + row]
    stat_kernel(flags, other_ref, stat_ref)
    mean, spread = stat_ref[0:1, :], stat_ref[1:2, :]
    away = (mean - first_ref[0:1, :]) * 0.5
    stat_ref[0:1, :] = (mean + first_ref[0:1, :]) * 0.5
    stat_ref[1:2, :] = (spread + first_ref[1:2, :]) * 0.5 + away * away


def affine(stat_ref, vector_ref, first):
    scale = lax.rsqrt(stat_ref[1:2, :] + EPS) * vector_ref[first : first + 1, :]
    return scale, vector_ref[first + 1 : first + 2, :] - stat_ref[0:1, :] * scale


def conv_kernel(
    flags,
    stat_ref,
    vector_ref,
    own_ref,
    past_ref,
    edge_ref,
    cross_ref,
    weight_ref,
    out0_ref,
    out1_ref,
    act_ref,
    acc_ref,
    tap_ref,
    sems,
):
    width, chans = own_ref.shape[2], own_ref.shape[3]
    later, parity = flags[0] == 1, flags[1]
    keep = {0: jnp.where(flags[2] > 0, 1.0, 0.0), 3: jnp.where(flags[3] > 0, 1.0, 0.0)}
    copies = [
        pltpu.make_async_copy(weight_ref.at[i], tap_ref.at[i], sems.at[i]) for i in range(9)
    ]
    for copy in copies:
        copy.start()
    scale, shift = affine(stat_ref, vector_ref, 0)
    half_scale, half_shift = scale * 0.5, shift * 0.5
    zero = jnp.zeros((1, chans), BF)

    def put(frame, row):
        if row in keep:
            at = jnp.maximum(2 * flags[0] - 2 + frame, 0)
            mine, theirs = edge_ref[at], cross_ref[at]
            raw = jnp.where(later, theirs, mine) if row == 0 else jnp.where(later, mine, theirs)
        elif frame >= 2:
            raw = own_ref[frame - 2, row - 1]
        else:
            raw = jnp.where(later, past_ref[frame, row - 1], own_ref[0, row - 1])
        raw = raw.astype(F32)
        half = raw * half_scale + half_shift
        act = half + half * jnp.tanh(half)
        if row in keep:
            act = act * keep[row]
        act = act.astype(BF)
        act_ref[frame, row, :, 0:chans] = jnp.concatenate([zero, act[: width - 1]], axis=0)
        act_ref[frame, row, :, chans : 2 * chans] = act
        act_ref[frame, row, :, 2 * chans : 3 * chans] = jnp.concatenate([act[1:], zero], axis=0)

    ready = set()
    for i in range(9):
        tap_t, tap_h = i // 3, i % 3
        for frame in (tap_t, tap_t + 1):
            for row in (tap_h, tap_h + 1):
                if (frame, row) not in ready:
                    ready.add((frame, row))
                    put(frame, row)
        copies[i].wait()
        slab = act_ref[tap_t : tap_t + 2, tap_h : tap_h + 2].reshape(4 * width, 3 * chans)
        part = jnp.dot(slab, tap_ref[i], preferred_element_type=F32).reshape(acc_ref.shape)
        if i == 0:
            acc_ref[...] = part
        else:
            acc_ref[...] += part

    outs = (out0_ref, out1_ref)
    for p in range(2):
        frame = (parity + p) & 1
        for h in range(2):
            value = own_ref[frame, h].astype(F32) + (acc_ref[frame, h] + vector_ref[2:3, :])
            outs[p][h * width : (h + 1) * width, :] = value.astype(BF)


def dot_t(a, b):
    return lax.dot_general(a, b, (((1,), (1,)), ((), ())), preferred_element_type=F32)


def gather(query, block, mask, state):
    score = dot_t(query, block)
    if mask is not None:
        score = score + mask
    top = jnp.max(score, axis=-1, keepdims=True)
    if state is not None:
        top = jnp.maximum(state[0], top)
    weight = jnp.exp2(score - top)
    total = jnp.sum(weight, axis=-1, keepdims=True)
    acc = jnp.dot(weight.astype(BF), block, preferred_element_type=F32)
    if state is not None:
        fade = jnp.exp2(state[0] - top)
        total = state[1] * fade + total
        acc = state[2] * fade + acc
    return top, total, acc


def keep_state(state, acc_ref, sum_ref):
    top, total, acc = state
    acc_ref[...] = acc
    lane = lax.broadcasted_iota(jnp.int32, sum_ref.shape, 1)
    sum_ref[...] = jnp.where(lane == 0, top, total)


def load_state(acc_ref, sum_ref):
    return sum_ref[:, 0:1], sum_ref[:, 1:2], acc_ref[...]


def reach_mask(flags, order, far_side, row, start, cells):
    core, low = flags[0], flags[1]
    side = core ^ far_side
    fine = jnp.where(side == 0, flags[4], flags[5])
    mask = 0.0
    for p in range(2):
        key_upper, query_upper = low ^ p, low ^ order
        seen = jnp.where(side == 0, key_upper >= query_upper, key_upper <= query_upper)
        here = (row >= start + p * cells) & (row < start + (p + 1) * cells)
        mask = mask + jnp.where(here & jnp.logical_not(seen & (fine > 0)), -1e30, 0.0)
    return mask


OWN_KEYS = 2944


def own_kernel(
    flags,
    stat_ref,
    vector_ref,
    mine_ref,
    swap_ref,
    near_ref,
    wq_ref,
    wk_ref,
    query0_ref,
    query1_ref,
    acc0_ref,
    acc1_ref,
    sum0_ref,
    sum1_ref,
    key_ref,
):
    cells, chans = query0_ref.shape
    scale, shift = affine(stat_ref, vector_ref, 3)
    for i, ref in enumerate((mine_ref, swap_ref, near_ref)):
        raw = ref[...].astype(F32)
        key_ref[2 * i * cells : 2 * (i + 1) * cells, :] = (raw * scale + shift).astype(BF)
    key_ref[6 * cells : OWN_KEYS, :] = jnp.zeros((OWN_KEYS - 6 * cells, chans), BF)
    factor = LOG2E / math.sqrt(chans)
    queries = (query0_ref, query1_ref)
    for p in range(2):
        normed = key_ref[p * cells : (p + 1) * cells, :]
        query = jnp.dot(normed, wq_ref[...], preferred_element_type=F32).astype(BF)
        queries[p][...] = (dot_t(query, wk_ref[...]) * factor).astype(BF)
    row = lax.broadcasted_iota(jnp.int32, (1, OWN_KEYS), 1)
    for p, (acc_ref, sum_ref) in enumerate(((acc0_ref, sum0_ref), (acc1_ref, sum1_ref))):
        mask = reach_mask(flags, p, 0, row, 4 * cells, cells)
        mask = mask + jnp.where(row >= 6 * cells, -1e30, 0.0)
        keep_state(gather(queries[p][...], key_ref[...], mask, None), acc_ref, sum_ref)


def tail_kernel(
    order,
    flags,
    stat_ref,
    vector_ref,
    far_ref,
    relay_ref,
    query_ref,
    acc_ref,
    sum_ref,
    own_ref,
    wv_ref,
    wo_ref,
    out_ref,
    key_ref,
):
    cells = out_ref.shape[0]
    scale, shift = affine(stat_ref, vector_ref, 3)
    for i, ref in enumerate((far_ref, relay_ref)):
        raw = ref[...].astype(F32)
        key_ref[2 * i * cells : 2 * (i + 1) * cells, :] = (raw * scale + shift).astype(BF)
    row = lax.broadcasted_iota(jnp.int32, (1, 4 * cells), 1)
    mask = reach_mask(flags, order, 1, row, 2 * cells, cells)
    far_ok = jnp.where(flags[0] == 0, flags[4], flags[5])
    mask = mask + jnp.where((row < 2 * cells) & (far_ok == 0), -1e30, 0.0)
    state = load_state(acc_ref, sum_ref)
    _, total, acc = gather(query_ref[...], key_ref[...], mask, state)
    mixed = (acc / total).astype(BF)
    attn = jnp.dot(mixed, wv_ref[...], preferred_element_type=F32).astype(BF)
    result = jnp.dot(attn, wo_ref[...], preferred_element_type=F32)
    own = own_ref[...].astype(F32)
    out_ref[...] = (own + vector_ref[5:6, :] + result).astype(BF)


def place_kernel(flags, back0_ref, back1_ref, out_ref):
    odd = flags[1]
    out_ref[odd] = back0_ref[...]
    out_ref[1 - odd] = back1_ref[...]


def whole():
    return pl.BlockSpec(memory_space=pltpu.VMEM)


def remote():
    return pl.BlockSpec(memory_space=pl.ANY)


def cost(flops, moved):
    return pl.CostEstimate(flops=int(flops), bytes_accessed=int(moved), transcendentals=0)


def flag_spec():
    return pl.BlockSpec(memory_space=pltpu.SMEM)


def params(mib):
    return pltpu.CompilerParams(vmem_limit_bytes=mib * 1024 * 1024)


def shards(
    feat,
    norm1_gain,
    norm1_bias,
    conv_weight,
    conv_bias,
    norm2_gain,
    norm2_bias,
    w_query,
    w_key,
    w_value,
    w_out,
    out_bias,
):
    frames, rows, width, chans = feat.shape
    t, z, x, y = (lax.axis_index(a) for a in AXES)
    block = z * NX + x
    stripe = block * NY + y
    i32 = lambda *v: jnp.stack([jnp.asarray(a, jnp.int32) for a in v])

    stat_shape = jax.ShapeDtypeStruct((2, chans), F32)
    flags = i32(t, y & 1, stripe > 0, stripe < NZ * NX * NY - 1, block > 0, block < NZ * NX - 1)
    vectors = jnp.stack([norm1_gain, norm1_bias, conv_bias, norm2_gain, norm2_bias, out_bias])
    swap = turned("tm", 1)
    stat_shape = jax.ShapeDtypeStruct((2, chans), F32)

    def stats_of(*pieces):
        return pl.pallas_call(
            stat_kernel,
            out_shape=stat_shape,
            in_specs=[flag_spec()] + [whole()] * len(pieces),
            out_specs=whole(),
            compiler_params=params(16),
            name="stats",
        )(flags, *[a.reshape(-1, width, chans) for a in pieces])

    other = send(feat, swap)
    row_shape = jax.ShapeDtypeStruct((2 * frames, width, chans), BF)
    first, kept, vectors = pl.pallas_call(
        first_kernel,
        out_shape=(stat_shape, row_shape, jax.ShapeDtypeStruct(vectors.shape, F32)),
        in_specs=[flag_spec(), whole(), whole()],
        out_specs=(whole(),) * 3,
        compiler_params=params(16),
        name="first",
    )(flags, feat.reshape(-1, width, chans), vectors)
    stats, edge = pl.pallas_call(
        edge_kernel,
        out_shape=(stat_shape, row_shape),
        in_specs=[flag_spec(), whole(), whole(), whole()],
        out_specs=(whole(), whole()),
        compiler_params=params(16),
        name="edges",
    )(flags, kept, other.reshape(-1, width, chans), first)
    edge = send(edge, edges_out)
    stats = over(over(stats, "z"), "x")
    edge, stats = lax.optimization_barrier((edge, stats))
    cross = send(edge, swap)
    stats = over(stats, "y")

    cells = rows * width
    piece = jax.ShapeDtypeStruct((cells, chans), BF)
    own0, own1 = pl.pallas_call(
        conv_kernel,
        out_shape=(piece, piece),
        in_specs=[flag_spec()] + [whole()] * 6 + [remote()],
        out_specs=(whole(),) * 2,
        scratch_shapes=[
            pltpu.VMEM((4, 4, width, 3 * chans), BF),
            pltpu.VMEM((frames, rows, width, chans), F32),
            pltpu.VMEM((9, 3 * chans, chans), BF),
            pltpu.SemaphoreType.DMA((9,)),
        ],
        compiler_params=params(CONV),
        cost_estimate=cost(27 * 2 * 960 * chans * chans, 20e6),
        name="conv",
    )(
        flags,
        stats,
        vectors,
        kept.reshape(feat.shape),
        other,
        edge,
        cross,
        conv_weight.reshape(9, 3 * chans, chans),
    )

    mine0 = send(own0, to_frames(0))
    mine1 = send(own1, to_frames(1))
    stats2 = stats_of(own0, own1)
    stats2 = over(over(stats2, "tm"), "z")
    mine = jnp.concatenate([mine0, mine1])
    swapped = send(mine, swap)
    near = send(after(mine, stats2), blocks_out)
    swapped, stats2 = lax.optimization_barrier((swapped, over(stats2, "x")))
    far = send(swapped, blocks_out)
    stats2 = over(stats2, "y")

    norm2 = (stats2, vectors)
    acc_shape = jax.ShapeDtypeStruct((cells, chans), F32)
    sum_shape = jax.ShapeDtypeStruct((cells, 128), F32)
    query0, query1, acc0, acc1, sum0, sum1 = pl.pallas_call(
        own_kernel,
        out_shape=(piece, piece, acc_shape, acc_shape, sum_shape, sum_shape),
        in_specs=[flag_spec()] + [whole()] * 7,
        out_specs=(whole(),) * 6,
        scratch_shapes=[pltpu.VMEM((OWN_KEYS, chans), BF)],
        compiler_params=params(OWN),
        cost_estimate=cost(6e9, 8e6),
        name="own",
    )(flags, *norm2, mine, swapped, near, w_query, w_key)
    relay = send(after(far, sum1), swap)

    def tail(order, query, acc, total, own):
        return pl.pallas_call(
            functools.partial(tail_kernel, order),
            out_shape=piece,
            in_specs=[flag_spec()] + [whole()] * 10,
            out_specs=whole(),
            scratch_shapes=[pltpu.VMEM((4 * cells, chans), BF)],
            compiler_params=params(TAIL),
            cost_estimate=cost(3e9, 5e6),
            name="tail%d" % order,
        )(
            flags,
            *norm2,
            far,
            relay,
            query,
            acc,
            total,
            own,
            w_value,
            w_out,
        )

    out0 = tail(0, query0, acc0, sum0, mine0)
    out1 = tail(1, query1, acc1, sum1, mine1)
    back0 = send(out0, to_stripes(0))
    back1 = send(out1, to_stripes(1))
    output = pl.pallas_call(
        place_kernel,
        out_shape=jax.ShapeDtypeStruct((frames, cells, chans), BF),
        in_specs=[flag_spec(), whole(), whole()],
        out_specs=whole(),
        compiler_params=params(8),
        name="place",
    )(flags, back0, back1)
    return output.reshape(feat.shape)


def solution(mesh):
    fine = Mesh(mesh.devices.reshape(2, NZ, NX, NY), AXES)
    place = P("tm", ("z", "x", "y"), None, None)
    return jax.shard_map(
        shards,
        mesh=fine,
        in_specs=(place,) + (P(),) * 11,
        out_specs=place,
        check_vma=False,
    )
```

```python
import functools
import math

import jax
import jax.numpy as jnp
import numpy as np
from jax import lax
from jax.experimental import pallas as pl
from jax.experimental.pallas import tpu as pltpu
from jax.sharding import Mesh, PartitionSpec as P

GROUPS = 32
EPS = 1e-06
AXES = ("tm", "z", "x", "y")
NZ, NX, NY = 4, 4, 4
LOG2E = 1.4426950408889634
CONV = 40
OWN = 24
TAIL = 24
BF = jnp.bfloat16
F32 = jnp.float32


def lin(t, z, x, y):
    return ((t * NZ + z) * NX + x) * NY + y


def pairs_of(move):
    found = []
    for t in range(2):
        for z in range(NZ):
            for x in range(NX):
                for y in range(NY):
                    dest = move(t, z, x, y)
                    if dest is not None:
                        found.append((lin(t, z, x, y), lin(*dest)))
    return found


def send(value, move):
    return lax.ppermute(value, AXES, pairs_of(move))


def edges_out(t, z, x, y):
    row = (z * NX + x) * NY + y + (1 - 2 * t)
    if 0 <= row < NZ * NX * NY:
        return (t, row // (NX * NY), (row // NY) % NX, row % NY)
    return None


def blocks_out(t, z, x, y):
    block = z * NX + x + (1 - 2 * t)
    if 0 <= block < NZ * NX:
        return (t, block // NX, block % NX, y)
    return None


def turned(axis, step):
    def move(t, z, x, y):
        if axis == "tm":
            return (1 - t, z, x, y)
        if axis == "z":
            return (t, (z + step) % NZ, x, y)
        if axis == "x":
            return (t, z, (x + step) % NX, y)
        return (t, z, x, (y + step) % NY)

    return move


def to_frames(order):
    def move(t, z, x, y):
        return (y // 2, z, x, 2 * t + ((y + order) & 1))

    return move


def to_stripes(order):
    forward = to_frames(order)
    back = {}
    for t in range(2):
        for y in range(NY):
            dest = forward(t, 0, 0, y)
            back[(dest[0], dest[3])] = (t, y)

    def move(t, z, x, y):
        there = back[(t, y)]
        return (there[0], z, x, there[1])

    return move


def merge(parts):
    count = len(parts)
    mid = sum(parts) / count
    away = [p[0:1] - mid[0:1] for p in parts]
    extra = sum(a * a for a in away) / count
    row = lax.broadcasted_iota(jnp.int32, mid.shape, 0)
    return mid + jnp.where(row == 1, jnp.broadcast_to(extra, mid.shape), 0.0)


def gathered(stats, axis):
    steps = (1,) if axis == "tm" else (1, 2, 3)
    return [stats] + [send(stats, turned(axis, k)) for k in steps]


def over(stats, axis):
    return merge(gathered(stats, axis))


def after(value, *first):
    return lax.optimization_barrier((value,) + first)[0]


def group_mean(row):
    chans = row.shape[-1]
    size = chans // GROUPS
    lane = lax.broadcasted_iota(jnp.int32, row.shape, 1)
    step = 1
    while step < size:
        low = (lane & step) == 0
        row = row + jnp.where(
            low, pltpu.roll(row, chans - step, 1), pltpu.roll(row, step, 1)
        )
        step *= 2
    return row / size


def local_stats(blocks, stat_ref):
    chans = stat_ref.shape[-1]
    cells = sum(b.shape[0] for b in [f() for f in blocks])
    total = sum(jnp.sum(f().astype(F32), axis=0, keepdims=True) for f in blocks)
    mean = group_mean(jnp.broadcast_to(total / cells, (8, chans)))
    center = mean[0:1]
    square = 0.0
    for f in blocks:
        away = f().astype(F32) - center
        square = square + jnp.sum(away * away, axis=0, keepdims=True)
    spread = group_mean(jnp.broadcast_to(square / cells, (8, chans)))
    stat_ref[0:1, :] = center
    stat_ref[1:2, :] = spread[0:1]


def stat_kernel(flags, *refs):
    local_stats(
        [functools.partial(lambda ref, i: ref[i], ref, i) for ref in refs[:-1] for i in range(ref.shape[0])],
        refs[-1],
    )


def first_kernel(flags, feat_ref, few_ref, stat_ref, kept_ref, vector_ref):
    kept_ref[...] = feat_ref[...]
    vector_ref[...] = few_ref[...]
    stat_kernel(flags, feat_ref, stat_ref)


def edge_kernel(flags, feat_ref, other_ref, first_ref, stat_ref, edge_ref):
    frames = feat_ref.shape[0] // 2
    core = flags[0]
    row = 1 - core
    for f in range(frames):
        edge_ref[frames * core + f] = feat_ref[2 * f + row]
        edge_ref[frames * (1 - core) + f] = other_ref[2 * f + row]
    stat_kernel(flags, other_ref, stat_ref)
    mean, spread = stat_ref[0:1, :], stat_ref[1:2, :]
    away = (mean - first_ref[0:1, :]) * 0.5
    stat_ref[0:1, :] = (mean + first_ref[0:1, :]) * 0.5
    stat_ref[1:2, :] = (spread + first_ref[1:2, :]) * 0.5 + away * away


def affine(stat_ref, vector_ref, first):
    scale = lax.rsqrt(stat_ref[1:2, :] + EPS) * vector_ref[first : first + 1, :]
    return scale, vector_ref[first + 1 : first + 2, :] - stat_ref[0:1, :] * scale


def conv_kernel(
    flags,
    stat_ref,
    vector_ref,
    own_ref,
    past_ref,
    edge_ref,
    cross_ref,
    weight_ref,
    out0_ref,
    out1_ref,
    act_ref,
    acc_ref,
    tap_ref,
    sems,
):
    width, chans = own_ref.shape[2], own_ref.shape[3]
    later, parity = flags[0] == 1, flags[1]
    keep = {0: jnp.where(flags[2] > 0, 1.0, 0.0), 3: jnp.where(flags[3] > 0, 1.0, 0.0)}
    copies = [
        pltpu.make_async_copy(weight_ref.at[i], tap_ref.at[i], sems.at[i]) for i in range(9)
    ]
    for copy in copies:
        copy.start()
    scale, shift = affine(stat_ref, vector_ref, 0)
    half_scale, half_shift = scale * 0.5, shift * 0.5
    zero = jnp.zeros((1, chans), BF)

    def put(frame, row):
        if row in keep:
            at = jnp.maximum(2 * flags[0] - 2 + frame, 0)
            mine, theirs = edge_ref[at], cross_ref[at]
            raw = jnp.where(later, theirs, mine) if row == 0 else jnp.where(later, mine, theirs)
        elif frame >= 2:
            raw = own_ref[frame - 2, row - 1]
        else:
            raw = jnp.where(later, past_ref[frame, row - 1], own_ref[0, row - 1])
        raw = raw.astype(F32)
        half = raw * half_scale + half_shift
        act = half + half * jnp.tanh(half)
        if row in keep:
            act = act * keep[row]
        act = act.astype(BF)
        act_ref[frame, row, :, 0:chans] = jnp.concatenate([zero, act[: width - 1]], axis=0)
        act_ref[frame, row, :, chans : 2 * chans] = act
        act_ref[frame, row, :, 2 * chans : 3 * chans] = jnp.concatenate([act[1:], zero], axis=0)

    ready = set()
    for i in range(9):
        tap_t, tap_h = i // 3, i % 3
        for frame in (tap_t, tap_t + 1):
            for row in (tap_h, tap_h + 1):
                if (frame, row) not in ready:
                    ready.add((frame, row))
                    put(frame, row)
        copies[i].wait()
        slab = act_ref[tap_t : tap_t + 2, tap_h : tap_h + 2].reshape(4 * width, 3 * chans)
        part = jnp.dot(slab, tap_ref[i], preferred_element_type=F32).reshape(acc_ref.shape)
        if i == 0:
            acc_ref[...] = part
        else:
            acc_ref[...] += part

    outs = (out0_ref, out1_ref)
    for p in range(2):
        frame = (parity + p) & 1
        for h in range(2):
            value = own_ref[frame, h].astype(F32) + (acc_ref[frame, h] + vector_ref[2:3, :])
            outs[p][h * width : (h + 1) * width, :] = value.astype(BF)


def dot_t(a, b):
    return lax.dot_general(a, b, (((1,), (1,)), ((), ())), preferred_element_type=F32)


def gather(query, block, mask, state):
    score = dot_t(query, block)
    if mask is not None:
        score = score + mask
    top = jnp.max(score, axis=-1, keepdims=True)
    if state is not None:
        top = jnp.maximum(state[0], top)
    weight = jnp.exp2(score - top)
    total = jnp.sum(weight, axis=-1, keepdims=True)
    acc = jnp.dot(weight.astype(BF), block, preferred_element_type=F32)
    if state is not None:
        fade = jnp.exp2(state[0] - top)
        total = state[1] * fade + total
        acc = state[2] * fade + acc
    return top, total, acc


def keep_state(state, acc_ref, sum_ref):
    top, total, acc = state
    acc_ref[...] = acc
    lane = lax.broadcasted_iota(jnp.int32, sum_ref.shape, 1)
    sum_ref[...] = jnp.where(lane == 0, top, total)


def load_state(acc_ref, sum_ref):
    return sum_ref[:, 0:1], sum_ref[:, 1:2], acc_ref[...]


def reach_mask(flags, order, far_side, row, start, cells):
    core, low = flags[0], flags[1]
    side = core ^ far_side
    fine = jnp.where(side == 0, flags[4], flags[5])
    mask = 0.0
    for p in range(2):
        key_upper, query_upper = low ^ p, low ^ order
        seen = jnp.where(side == 0, key_upper >= query_upper, key_upper <= query_upper)
        here = (row >= start + p * cells) & (row < start + (p + 1) * cells)
        mask = mask + jnp.where(here & jnp.logical_not(seen & (fine > 0)), -1e30, 0.0)
    return mask


OWN_KEYS = 2944


def own_kernel(
    flags,
    stat_ref,
    vector_ref,
    mine_ref,
    swap_ref,
    near_ref,
    wq_ref,
    wk_ref,
    query0_ref,
    query1_ref,
    acc0_ref,
    acc1_ref,
    sum0_ref,
    sum1_ref,
    key_ref,
):
    cells, chans = query0_ref.shape
    scale, shift = affine(stat_ref, vector_ref, 3)
    for i, ref in enumerate((mine_ref, swap_ref, near_ref)):
        raw = ref[...].astype(F32)
        key_ref[2 * i * cells : 2 * (i + 1) * cells, :] = (raw * scale + shift).astype(BF)
    key_ref[6 * cells : OWN_KEYS, :] = jnp.zeros((OWN_KEYS - 6 * cells, chans), BF)
    factor = LOG2E / math.sqrt(chans)
    queries = (query0_ref, query1_ref)
    for p in range(2):
        normed = key_ref[p * cells : (p + 1) * cells, :]
        query = jnp.dot(normed, wq_ref[...], preferred_element_type=F32).astype(BF)
        queries[p][...] = (dot_t(query, wk_ref[...]) * factor).astype(BF)
    row = lax.broadcasted_iota(jnp.int32, (1, OWN_KEYS), 1)
    for p, (acc_ref, sum_ref) in enumerate(((acc0_ref, sum0_ref), (acc1_ref, sum1_ref))):
        mask = reach_mask(flags, p, 0, row, 4 * cells, cells)
        mask = mask + jnp.where(row >= 6 * cells, -1e30, 0.0)
        keep_state(gather(queries[p][...], key_ref[...], mask, None), acc_ref, sum_ref)


def tail_kernel(
    order,
    flags,
    stat_ref,
    vector_ref,
    far_ref,
    relay_ref,
    query_ref,
    acc_ref,
    sum_ref,
    own_ref,
    wv_ref,
    wo_ref,
    out_ref,
    key_ref,
):
    cells = out_ref.shape[0]
    scale, shift = affine(stat_ref, vector_ref, 3)
    for i, ref in enumerate((far_ref, relay_ref)):
        raw = ref[...].astype(F32)
        key_ref[2 * i * cells : 2 * (i + 1) * cells, :] = (raw * scale + shift).astype(BF)
    row = lax.broadcasted_iota(jnp.int32, (1, 4 * cells), 1)
    mask = reach_mask(flags, order, 1, row, 2 * cells, cells)
    far_ok = jnp.where(flags[0] == 0, flags[4], flags[5])
    mask = mask + jnp.where((row < 2 * cells) & (far_ok == 0), -1e30, 0.0)
    state = load_state(acc_ref, sum_ref)
    _, total, acc = gather(query_ref[...], key_ref[...], mask, state)
    mixed = (acc / total).astype(BF)
    attn = jnp.dot(mixed, wv_ref[...], preferred_element_type=F32).astype(BF)
    result = jnp.dot(attn, wo_ref[...], preferred_element_type=F32)
    own = own_ref[...].astype(F32)
    out_ref[...] = (own + vector_ref[5:6, :] + result).astype(BF)


def place_kernel(flags, back0_ref, back1_ref, out_hbm, sems):
    odd = flags[1]
    copies = [
        pltpu.make_async_copy(back0_ref, out_hbm.at[odd], sems.at[0]),
        pltpu.make_async_copy(back1_ref, out_hbm.at[1 - odd], sems.at[1]),
    ]
    for copy in copies:
        copy.start()
    for copy in copies:
        copy.wait()


def whole():
    return pl.BlockSpec(memory_space=pltpu.VMEM)


def remote():
    return pl.BlockSpec(memory_space=pl.ANY)


def cost(flops, moved):
    return pl.CostEstimate(flops=int(flops), bytes_accessed=int(moved), transcendentals=0)


def flag_spec():
    return pl.BlockSpec(memory_space=pltpu.SMEM)


def params(mib):
    return pltpu.CompilerParams(vmem_limit_bytes=mib * 1024 * 1024)


def shards(
    feat,
    norm1_gain,
    norm1_bias,
    conv_weight,
    conv_bias,
    norm2_gain,
    norm2_bias,
    w_query,
    w_key,
    w_value,
    w_out,
    out_bias,
):
    frames, rows, width, chans = feat.shape
    t, z, x, y = (lax.axis_index(a) for a in AXES)
    block = z * NX + x
    stripe = block * NY + y
    i32 = lambda *v: jnp.stack([jnp.asarray(a, jnp.int32) for a in v])

    stat_shape = jax.ShapeDtypeStruct((2, chans), F32)
    flags = i32(t, y & 1, stripe > 0, stripe < NZ * NX * NY - 1, block > 0, block < NZ * NX - 1)
    vectors = jnp.stack([norm1_gain, norm1_bias, conv_bias, norm2_gain, norm2_bias, out_bias])
    swap = turned("tm", 1)
    stat_shape = jax.ShapeDtypeStruct((2, chans), F32)

    def stats_of(*pieces):
        return pl.pallas_call(
            stat_kernel,
            out_shape=stat_shape,
            in_specs=[flag_spec()] + [whole()] * len(pieces),
            out_specs=whole(),
            compiler_params=params(16),
            name="stats",
        )(flags, *[a.reshape(-1, width, chans) for a in pieces])

    other = send(feat, swap)
    row_shape = jax.ShapeDtypeStruct((2 * frames, width, chans), BF)
    first, kept, vectors = pl.pallas_call(
        first_kernel,
        out_shape=(stat_shape, row_shape, jax.ShapeDtypeStruct(vectors.shape, F32)),
        in_specs=[flag_spec(), whole(), whole()],
        out_specs=(whole(),) * 3,
        compiler_params=params(16),
        name="first",
    )(flags, feat.reshape(-1, width, chans), vectors)
    stats, edge = pl.pallas_call(
        edge_kernel,
        out_shape=(stat_shape, row_shape),
        in_specs=[flag_spec(), whole(), whole(), whole()],
        out_specs=(whole(), whole()),
        compiler_params=params(16),
        name="edges",
    )(flags, kept, other.reshape(-1, width, chans), first)
    edge = send(edge, edges_out)
    stats = over(over(stats, "z"), "x")
    edge, stats = lax.optimization_barrier((edge, stats))
    cross = send(edge, swap)
    stats = over(stats, "y")

    cells = rows * width
    piece = jax.ShapeDtypeStruct((cells, chans), BF)
    own0, own1 = pl.pallas_call(
        conv_kernel,
        out_shape=(piece, piece),
        in_specs=[flag_spec()] + [whole()] * 6 + [remote()],
        out_specs=(whole(),) * 2,
        scratch_shapes=[
            pltpu.VMEM((4, 4, width, 3 * chans), BF),
            pltpu.VMEM((frames, rows, width, chans), F32),
            pltpu.VMEM((9, 3 * chans, chans), BF),
            pltpu.SemaphoreType.DMA((9,)),
        ],
        compiler_params=params(CONV),
        cost_estimate=cost(27 * 2 * 960 * chans * chans, 20e6),
        name="conv",
    )(
        flags,
        stats,
        vectors,
        kept.reshape(feat.shape),
        other,
        edge,
        cross,
        conv_weight.reshape(9, 3 * chans, chans),
    )

    mine0 = send(own0, to_frames(0))
    mine1 = send(own1, to_frames(1))
    stats2 = stats_of(own0, own1)
    stats2 = over(over(stats2, "tm"), "z")
    mine = jnp.concatenate([mine0, mine1])
    swapped = send(mine, swap)
    near = send(after(mine, stats2), blocks_out)
    swapped, stats2 = lax.optimization_barrier((swapped, over(stats2, "x")))
    far = send(swapped, blocks_out)
    stats2 = over(stats2, "y")

    norm2 = (stats2, vectors)
    acc_shape = jax.ShapeDtypeStruct((cells, chans), F32)
    sum_shape = jax.ShapeDtypeStruct((cells, 128), F32)
    query0, query1, acc0, acc1, sum0, sum1 = pl.pallas_call(
        own_kernel,
        out_shape=(piece, piece, acc_shape, acc_shape, sum_shape, sum_shape),
        in_specs=[flag_spec()] + [whole()] * 7,
        out_specs=(whole(),) * 6,
        scratch_shapes=[pltpu.VMEM((OWN_KEYS, chans), BF)],
        compiler_params=params(OWN),
        cost_estimate=cost(6e9, 8e6),
        name="own",
    )(flags, *norm2, mine, swapped, near, w_query, w_key)
    relay = send(after(far, sum1), swap)

    def tail(order, query, acc, total, own):
        return pl.pallas_call(
            functools.partial(tail_kernel, order),
            out_shape=piece,
            in_specs=[flag_spec()] + [whole()] * 10,
            out_specs=whole(),
            scratch_shapes=[pltpu.VMEM((4 * cells, chans), BF)],
            compiler_params=params(TAIL),
            cost_estimate=cost(3e9, 5e6),
            name="tail%d" % order,
        )(
            flags,
            *norm2,
            far,
            relay,
            query,
            acc,
            total,
            own,
            w_value,
            w_out,
        )

    out0 = tail(0, query0, acc0, sum0, mine0)
    out1 = tail(1, query1, acc1, sum1, mine1)
    back0 = send(out0, to_stripes(0))
    back1 = send(out1, to_stripes(1))
    output = pl.pallas_call(
        place_kernel,
        out_shape=jax.ShapeDtypeStruct((frames, cells, chans), BF),
        in_specs=[flag_spec(), whole(), whole()],
        out_specs=remote(),
        scratch_shapes=[pltpu.SemaphoreType.DMA((2,))],
        compiler_params=params(8),
        name="place",
    )(flags, back0, back1)
    return output.reshape(feat.shape)


def solution(mesh):
    fine = Mesh(mesh.devices.reshape(2, NZ, NX, NY), AXES)
    place = P("tm", ("z", "x", "y"), None, None)
    return jax.shard_map(
        shards,
        mesh=fine,
        in_specs=(place,) + (P(),) * 11,
        out_specs=place,
        check_vma=False,
    )
```
